256 devices in a mesh: seq: 16 (over z, x_lo), wr: 4 (over y), wc: 4 (over x_hi, core).
Axes of the slice: x: 4 (x_hi: 2, x_lo: 2; x = x_hi * 2 + x_lo), y: 4, z: 8, core: 2. Of those that a mesh axis runs over, the one named last changes fastest.
Arguments:
- tokens: bfloat16 [8192, 2048], P('seq', ('wr', 'wc')), may hold values from -6 to 6
- ln_gain: float32 [2, 2048], replicated, may hold values from 0.5 to 1.5
- w_branch: bfloat16 [2, 2048, 4096], P(None, None, ('wr', 'wc')), may hold values from -0.125 to 0.125
- w_outgate: bfloat16 [2, 2048, 4096], P(None, None, ('wr', 'wc')), may hold values from -0.125 to 0.125
- w_gates: bfloat16 [2, 2048, 8], replicated, may hold values from -0.125 to 0.125
- forget_bias: float32 [2, 4], replicated, may hold values from 3.2 to 11
- conv_weight: float32 [2, 4, 4096], P(None, None, ('wr', 'wc')), may hold values from -3 to 3
- conv_bias: float32 [2, 4096], P(None, ('wr', 'wc')), may hold values from -3 to 3
- w_query: float32 [2, 4, 4, 4, 256], P(None, 'wr'), may hold values from -3 to 3
- w_key: float32 [2, 4, 4, 4, 256], P(None, 'wr'), may hold values from -3 to 3
- w_value: float32 [2, 4, 4, 4, 256], P(None, 'wr', None, 'wc'), may hold values from -4 to 4
- skip_gain: float32 [2, 4096], P(None, ('wr', 'wc')), may hold values from 0.5 to 1.5
- norm_gain: float32 [2, 4096], P(None, ('wr', 'wc')), may hold values from 0.5 to 1.5
- w_down: bfloat16 [2, 4096, 2048], P(None, ('wr', 'wc')), may hold values from -0.125 to 0.125
- lengths: int32 [3], replicated, may hold values from 1 to 4096, 8192 in all
- request_prompt: int32 [32], P('seq'), may hold values from 0 to 2
Outputs:
- mixed: bfloat16 [8192, 2048], P('seq', ('wr', 'wc'))
- request_state: bfloat16 [2, 32, 4, 1024, 1024], P(None, 'seq', 'wr', None, 'wc')
- request_conv: bfloat16 [2, 32, 3, 4096], P(None, 'seq', None, ('wr', 'wc'))
The draws below stay inside these ranges and needn't reach their ends.
Inputs may be any that keep to these rules, and one draw needn't show every extreme that they name: `lengths`: the 3 prompts lie end to end in order and fill all 8192 positions; the longest has exactly 4096 positions.
All inputs are finite; a program needn't handle non-finite values.
Results may differ from the reference program's by a relative error of at most 0.035.
Values may be sent and summed in bfloat16 or wider, within the bound.
A program may use at most 128 MiB of HBM per device.

```python
import math
import jax
import jax.numpy as jnp
import numpy as np
from jax import lax

D = 2048
INNER = 4096
HEADS = 4
CONV = 4
LAYERS = 2
BLK = 512
PROMPTS = 3
TOK_DEV = 512
QB = 256
TOKENS = 8192
REQS = 32
MOSTLEN = 4096
N_WR = 4
N_WC = 4


def draw_forget_bias(key, part):
    slow_key, fast_key, pick_key = jax.random.split(key, 3)
    slow_rate = jax.random.uniform(slow_key, (LAYERS, HEADS), jnp.float32, 9.0, 11.0)
    fast_rate = jax.random.uniform(fast_key, (LAYERS, HEADS), jnp.float32, 3.2, 5.0)
    chooser = jax.random.uniform(pick_key, (LAYERS, HEADS), jnp.float32)
    picked = jnp.where(chooser < 0.5, slow_rate, fast_rate)
    return picked


def draw_w_value(key, part):
    base_key = jax.random.fold_in(key, 0)
    draw_shape = (LAYERS, HEADS, 4, 4, QB)
    column = jnp.arange(4, dtype=jnp.float32).reshape(1, 1, 1, 4, 1)
    rising = 0.6 + 0.4 * column
    sampled = 0.5 * jax.random.normal(base_key, draw_shape, jnp.float32) * rising
    return jnp.clip(sampled, -4.0, 4.0)


def with_ends(entries, rng, smallest, top_value):
    index_at = [jax.random.randint(jax.random.fold_in(rng, axis), (), 0, length) for axis, length in enumerate(entries.shape)]
    widest = entries.shape.index(max(entries.shape))
    neighbour = index_at[:widest] + [(index_at[widest] + 1) % entries.shape[widest]] + index_at[widest + 1:]
    return entries.at[tuple(index_at)].set(smallest).at[tuple(neighbour)].set(top_value)


def strengthened(drawn, stream_key, source, target, shards_of, factor):
    def block_of(position):
        return (jnp.arange(drawn.shape[position]) // (drawn.shape[position] // shards_of)).reshape((-1,) + (1,) * (drawn.ndim - 1 - position))

    first = jax.random.permutation(stream_key, shards_of)[block_of(target)]
    far = (block_of(target) + shards_of // 2) % shards_of
    return jnp.where((block_of(source) == first) | (block_of(source) == far), factor * drawn, drawn)


def shard_levels(rng, shape, pieces, least, high):
    level = 1.0
    for dim, blocks in pieces:
        heights = jax.random.uniform(jax.random.fold_in(jax.random.fold_in(rng, 6), dim), (blocks,), jnp.float32, least / len(pieces), high / len(pieces))
        level = level * jnp.repeat(jnp.exp(heights), shape[dim] // blocks).reshape((-1,) + (1,) * (len(shape) - 1 - dim))
    return level


def profile(count, total, limit, lean):
    weights = [(1 << 20) // math.isqrt(standing ** lean) + 1 for standing in range(2, count + 1)]
    surplus, given = total - limit - (count - 1), [1] * (count - 1)
    while surplus > 0:
        free = [i for i in range(count - 1) if given[i] < limit]
        whole, left = sum([weights[i] for i in free]), surplus
        for i in free:
            more = min(limit - given[i], max(1, left * weights[i] // whole), surplus)
            given[i] = given[i] + more
            surplus = surplus - more
    return np.array([limit] + given)


def ragged(key, amount, total, most, slope):
    if amount == 2:
        one = jax.random.randint(key, (), max(1, total - most), min(most, total - 1) + 1)
        return jnp.stack([one, total - one])
    sizes = jnp.asarray(profile(amount, total, most, slope), jnp.int32)
    twos = (amount - 1) // 2
    source_of, taker = sizes[1:1 + 2 * twos:2], sizes[2:2 + 2 * twos:2]
    slack = jnp.minimum(source_of - 1, most - taker)
    moved = jax.random.randint(jax.random.fold_in(key, 1), (twos,), 0, 1 << 20) % (slack + 1)
    sizes = sizes.at[1:1 + 2 * twos:2].set(source_of - moved).at[2:2 + 2 * twos:2].set(taker + moved)
    return sizes[jax.random.permutation(jax.random.fold_in(key, 2), amount)]


def scatter_about(stream_key, extent, deviation, limit, cuts=(), kind=jnp.bfloat16):
    result = jax.random.normal(stream_key, extent, jnp.float32) * deviation
    if len(cuts) > 0:
        result = shard_levels(stream_key, extent, cuts, -0.22, 0.18) * result
    return jnp.clip(result, min=-limit, max=limit).astype(kind)


def gaussian_with(own_key, extent, scale, limit, cuts, heavy, kind=jnp.bfloat16):
    result = scale * jax.random.normal(own_key, extent, jnp.float32)
    if cuts:
        result = result * shard_levels(own_key, extent, cuts, -0.22, 0.18)
    return jnp.clip(strengthened(result, jax.random.fold_in(own_key, 3), *heavy), -limit, limit).astype(kind)


def setup_inputs(seed: int = 0) -> dict:
    splits = jax.random.split(jax.random.key(seed), 17)
    tokens = scatter_about(splits[0], (TOKENS, D), 1.0, 6.0, ((0, 16), (1, 16)))
    ln_gain = jnp.clip(1.0 + 0.1 * jax.random.normal(splits[1], (LAYERS, D), jnp.float32), 0.5, 1.5)
    w_branch = scatter_about(splits[2], (LAYERS, D, INNER), D ** -0.5, 0.125, ((2, 16),))
    w_outgate = scatter_about(splits[3], (LAYERS, D, INNER), D ** -0.5, 0.125, ((2, 16),))
    w_gates = scatter_about(splits[4], (LAYERS, D, 2 * HEADS), D ** -0.5, 0.125)
    forget_bias = draw_forget_bias(jax.random.fold_in(splits[16], 71), 0)
    conv_weight = scatter_about(splits[6], (LAYERS, CONV, INNER), CONV ** -0.5, 3.0, ((2, 16),), jnp.float32)
    conv_bias = scatter_about(splits[7], (LAYERS, INNER), 0.5, 3.0, ((1, 16),), jnp.float32)
    w_query = scatter_about(splits[8], (LAYERS, HEADS, 4, 4, QB), 4 ** -0.5, 3.0, ((1, 4),), jnp.float32)
    w_key = scatter_about(splits[9], (LAYERS, HEADS, 4, 4, QB), 4 ** -0.5, 3.0, ((1, 4),), jnp.float32)
    w_value = draw_w_value(jax.random.fold_in(splits[16], 71), 0)
    skip_gain = jnp.clip(1.0 + 0.1 * jax.random.normal(splits[11], (LAYERS, INNER), jnp.float32), 0.5, 1.5)
    norm_gain = jnp.clip(1.0 + 0.1 * jax.random.normal(splits[12], (LAYERS, INNER), jnp.float32), 0.5, 1.5)
    w_down = gaussian_with(splits[13], (LAYERS, INNER, D), INNER ** -0.5, 0.125, ((1, 16),), (1, 2, 16, 2.0))
    lengths = ragged(splits[14], PROMPTS, TOKENS, MOSTLEN, 1).astype(jnp.int32)
    request_prompt = with_ends(jax.random.randint(splits[15], (REQS,), 0, PROMPTS), jax.random.fold_in(splits[15], 1), 0, PROMPTS - 1).astype(jnp.int32)
    return {"tokens": tokens, "ln_gain": ln_gain, "w_branch": w_branch, "w_outgate": w_outgate, "w_gates": w_gates, "forget_bias": forget_bias, "conv_weight": conv_weight, "conv_bias": conv_bias, "w_query": w_query, "w_key": w_key, "w_value": w_value, "skip_gain": skip_gain, "norm_gain": norm_gain, "w_down": w_down, "lengths": lengths, "request_prompt": request_prompt}


EPSILON = 1e-05
GATE_CAP = 15.0
ROW_DIMS = (((0,), (0,)), ((), ()))
FEATURE_DIMS = (((1,), (1,)), ((), ()))

def norm_rows(source, gain_row):
    widened = source.astype(jnp.float32)
    row_mean = lax.optimization_barrier(jnp.mean(widened, axis=1, keepdims=True))
    row_var = lax.optimization_barrier(jnp.mean(widened * widened, axis=1, keepdims=True)) - row_mean * row_mean
    return ((widened - row_mean) * lax.rsqrt(row_var + EPSILON) * gain_row).astype(jnp.bfloat16)

def segment_of(positions, lengths):
    bound_one = lengths[0]
    bound_two = lengths[0] + lengths[1]
    return (positions >= bound_one).astype(jnp.int32) + (positions >= bound_two).astype(jnp.int32)

def conv_rows(extended, ext_segment, segment, weight, bias_row):
    row_count = segment.shape[0]
    widened = extended.astype(jnp.float32)
    summed = jnp.zeros((row_count, widened.shape[1]), jnp.float32) + bias_row
    for back_step in range(weight.shape[0]):
        low_row = weight.shape[0] - 1 - back_step
        keep_row = (ext_segment[low_row:low_row + row_count] == segment).astype(jnp.float32)
        summed = summed + weight[back_step] * widened[low_row:low_row + row_count] * keep_row[:, None]
    return jax.nn.silu(summed).astype(jnp.bfloat16)

def block_mix(source, weight):
    row_count = source.shape[0]
    grouped = source.astype(jnp.float32).reshape(row_count, 4, -1)
    mixed = jnp.einsum('tig,ijg->tjg', grouped, weight.astype(jnp.float32), precision=lax.Precision.HIGHEST)
    return mixed.reshape(row_count, -1)

def block_terms(queries, key_rows, values, log_forget, in_gate, segment, prev_seg):
    row_count = queries.shape[0]
    cum_log = jnp.cumsum(log_forget)
    row_order = jnp.arange(row_count)
    allowed = (row_order[:, None] >= row_order[None, :]) & (segment[:, None] == segment[None, :])
    exponent = jnp.where(allowed, cum_log[:, None] - cum_log[None, :] + in_gate[None, :], -jnp.inf)
    scores = lax.dot_general(queries, key_rows, FEATURE_DIMS, preferred_element_type=jnp.float32) * jnp.exp(exponent)
    in_block = jnp.dot(scores.astype(jnp.bfloat16), values, preferred_element_type=jnp.float32)
    carried = jnp.where(segment == prev_seg, jnp.exp(cum_log), 0.0)
    last_seg = segment[row_count - 1]
    weights = jnp.where(segment == last_seg, jnp.exp(cum_log[row_count - 1] - cum_log + in_gate), 0.0)
    weighted = (key_rows.astype(jnp.float32) * weights[:, None]).astype(jnp.bfloat16)
    increment = lax.dot_general(weighted, values, ROW_DIMS, preferred_element_type=jnp.float32)
    block_decay = jnp.where(last_seg == prev_seg, jnp.exp(cum_log[row_count - 1]), 0.0)
    return (in_block, carried, increment, block_decay)

def end_state(state_in, key_rows, values, cum_log, in_gate, segment, seg_before, local_end, prompt, holder):
    end_cum = cum_log[local_end]
    entering = jnp.where(holder & (seg_before == prompt), jnp.exp(end_cum), 0.0)
    row_order = jnp.arange(segment.shape[0])
    chosen = holder & (segment == prompt) & (row_order <= local_end)
    weights = jnp.where(chosen, jnp.exp(end_cum - cum_log + in_gate), 0.0)
    weighted = (key_rows.astype(jnp.float32) * weights[:, None]).astype(jnp.bfloat16)
    return entering * state_in + lax.dot_general(weighted, values, ROW_DIMS, preferred_element_type=jnp.float32)

def mlstm_head(queries, key_rows, values, log_forget, in_gate, segment):
    block_count = queries.shape[0] // BLK
    seg_blocks = segment.reshape(block_count, BLK)
    prev_segs = jnp.concatenate([jnp.full((1,), -1, jnp.int32), seg_blocks[:-1, BLK - 1]])

    def advance(state_now, inputs):
        block_queries, block_keys, block_values, block_log, block_gate, block_seg, prev_seg = inputs
        in_block, carried, increment, block_decay = block_terms(block_queries, block_keys, block_values, block_log, block_gate, block_seg, prev_seg)
        hidden = in_block + carried[:, None] * jnp.dot(block_queries, state_now.astype(jnp.bfloat16), preferred_element_type=jnp.float32)
        return (block_decay * state_now + increment, (hidden, state_now))
    initial = jnp.zeros((key_rows.shape[1], values.shape[1]), jnp.float32)
    final_carry, (hidden, block_states) = lax.scan(advance, initial, (queries.reshape(block_count, BLK, -1), key_rows.reshape(block_count, BLK, -1), values.reshape(block_count, BLK, -1), log_forget.reshape(block_count, BLK), in_gate.reshape(block_count, BLK), seg_blocks, prev_segs))
    return (hidden.reshape(queries.shape[0], values.shape[1]), block_states)

def reference(tokens, ln_gain, w_branch, w_outgate, w_gates, forget_bias, conv_weight, conv_bias, w_query, w_key, w_value, skip_gain, norm_gain, w_down, lengths, request_prompt):
    total_rows = tokens.shape[0]
    positions = jnp.arange(total_rows, dtype=jnp.int32)
    segment = segment_of(positions, lengths)
    ext_segment = jnp.concatenate([jnp.full((CONV - 1,), -1, jnp.int32), segment])
    prompt_starts = [jnp.zeros((), jnp.int32), lengths[0], lengths[0] + lengths[1]]
    prompt_ends = [lengths[0] - 1, lengths[0] + lengths[1] - 1, jnp.zeros((), jnp.int32) + (total_rows - 1)]
    head_width = INNER // HEADS
    slab_width = INNER // (N_WR * N_WC)
    dev_blocks = TOK_DEV // BLK
    current = tokens
    state_layers = []
    edge_layers = []
    for layer_idx in range(LAYERS):
        normed = norm_rows(current, ln_gain[layer_idx])
        branch = jnp.dot(normed, w_branch[layer_idx], preferred_element_type=jnp.float32).astype(jnp.bfloat16)
        outgate = jnp.dot(normed, w_outgate[layer_idx], preferred_element_type=jnp.float32)
        gate_pre = jnp.dot(normed, w_gates[layer_idx], preferred_element_type=jnp.float32)
        padded_branch = jnp.concatenate([jnp.zeros((CONV - 1, INNER), jnp.bfloat16), branch], axis=0)
        conv_act = conv_rows(padded_branch, ext_segment, segment, conv_weight[layer_idx], conv_bias[layer_idx])
        normal_heads = []
        prompt_states = [[] for prompt in range(PROMPTS)]
        for head_idx in range(HEADS):
            lo_col = head_idx * head_width
            hi_col = lo_col + head_width
            queries = block_mix(conv_act[:, lo_col:hi_col], w_query[layer_idx, head_idx]).astype(jnp.bfloat16)
            key_rows = (block_mix(conv_act[:, lo_col:hi_col], w_key[layer_idx, head_idx]) * head_width ** (-0.5)).astype(jnp.bfloat16)
            values = block_mix(branch[:, lo_col:hi_col], w_value[layer_idx, head_idx]).astype(jnp.bfloat16)
            in_gate = GATE_CAP * jnp.tanh(gate_pre[:, head_idx] / GATE_CAP)
            log_forget = jax.nn.log_sigmoid(gate_pre[:, HEADS + head_idx] + forget_bias[layer_idx, head_idx])
            hidden, block_states = mlstm_head(queries, key_rows, values, log_forget, in_gate, segment)
            sums_one = lax.optimization_barrier(jnp.sum(hidden, axis=1))
            sums_two = lax.optimization_barrier(jnp.sum(hidden * hidden, axis=1))
            row_mean = sums_one / head_width
            row_var = sums_two / head_width - row_mean * row_mean
            normal_heads.append((hidden - row_mean[:, None]) * lax.rsqrt(row_var + EPSILON)[:, None])
            for prompt in range(PROMPTS):
                end_pos = prompt_ends[prompt]
                device = end_pos // TOK_DEV
                dev_start = (device * TOK_DEV).astype(jnp.int32)
                state_in = block_states[device * dev_blocks]
                seg_before = jnp.where(dev_start > 0, segment[jnp.maximum(dev_start - 1, 0)], -1)
                part_log = lax.dynamic_slice_in_dim(log_forget, dev_start, TOK_DEV, 0)
                part_gate = lax.dynamic_slice_in_dim(in_gate, dev_start, TOK_DEV, 0)
                part_seg = lax.dynamic_slice_in_dim(segment, dev_start, TOK_DEV, 0)
                part_keys = lax.dynamic_slice_in_dim(key_rows, dev_start, TOK_DEV, 0)
                part_values = lax.dynamic_slice_in_dim(values, dev_start, TOK_DEV, 0)
                cum_log = jnp.cumsum(part_log)
                holder = end_pos >= dev_start
                prompt_states[prompt].append(end_state(state_in, part_keys, part_values, cum_log, part_gate, part_seg, seg_before, (end_pos - dev_start).astype(jnp.int32), prompt, holder))
        normal_all = jnp.concatenate(normal_heads, axis=1)
        gated = ((normal_all * norm_gain[layer_idx] + skip_gain[layer_idx] * conv_act.astype(jnp.float32)) * jax.nn.silu(outgate)).astype(jnp.bfloat16)
        accum = jnp.zeros((total_rows, D), jnp.float32)
        for block_idx in range(N_WR * N_WC):
            lo_row = block_idx * slab_width
            product = jnp.dot(gated[:, lo_row:lo_row + slab_width], w_down[layer_idx, lo_row:lo_row + slab_width], preferred_element_type=jnp.float32)
            rounded = lax.optimization_barrier(product.astype(jnp.bfloat16))
            accum = accum + rounded.astype(jnp.float32)
        current = (current.astype(jnp.float32) + accum).astype(jnp.bfloat16)
        finals = jnp.stack([jnp.stack(prompt_states[prompt]) for prompt in range(PROMPTS)]).astype(jnp.bfloat16)
        edges = []
        for prompt in range(PROMPTS):
            end_pos = prompt_ends[prompt]
            window = lax.dynamic_slice_in_dim(padded_branch, (end_pos + 1).astype(jnp.int32), CONV - 1, 0)
            edge_pos = end_pos - (CONV - 2) + jnp.arange(CONV - 1, dtype=jnp.int32)
            edges.append(jnp.where((edge_pos >= prompt_starts[prompt])[:, None], window, jnp.zeros_like(window)))
        edge_stack = jnp.stack(edges)
        state_layers.append(jnp.take(finals, request_prompt, axis=0))
        edge_layers.append(jnp.take(edge_stack, request_prompt, axis=0))
    return (current, jnp.stack(state_layers), jnp.stack(edge_layers))
```

```python
import jax
import jax.numpy as jnp
from jax import lax
from jax.experimental import pallas as pl
from jax.experimental.pallas import tpu as pltpu
from jax.sharding import PartitionSpec as P

HEADS = 4
CONV = 4
LAYERS = 2
PROMPTS = 3
SEQ = 16
SPLIT = 7

EPSILON = 1e-05
GATE_CAP = 15.0
FEATURE_DIMS = (((1,), (1,)), ((), ()))
ROW_DIMS = (((0,), (0,)), ((), ()))
MESH = pl.DeviceIdType.MESH
VM = pl.BlockSpec(memory_space=pltpu.VMEM)
DMA = pltpu.SemaphoreType.DMA


def params(collective):
    return pltpu.CompilerParams(
        collective_id=collective, has_side_effects=True, vmem_limit_bytes=48 * 1024 * 1024
    )


def greet(peers):
    barrier = pltpu.get_barrier_semaphore()
    for peer in peers:
        pl.semaphore_signal(barrier, inc=1, device_id=peer, device_id_type=MESH)
    pl.semaphore_wait(barrier, len(peers))


def copy_to(source, target, send, recv, peer):
    made = pltpu.make_async_remote_copy(
        src_ref=source, dst_ref=target, send_sem=send, recv_sem=recv, device_id=peer, device_id_type=MESH
    )
    made.start()
    return made


def plane():
    row, col = lax.axis_index("wr"), lax.axis_index("wc")
    core = lax.rem(col, 2)
    cross = lax.rem(col + 2, 4)
    mate = col + 1 - 2 * core
    return row, col, core, cross, mate


def plane_peers(row, cross, mate):
    return [{"wr": lax.rem(row + d, 4)} for d in (1, 2, 3)] + [{"wc": cross}, {"wc": mate}]


def gather_plane(own_ref, out_ref, send, recv):
    row, col, core, cross, mate = plane()
    mate_cross = lax.rem(mate + 2, 4)
    width = own_ref.shape[1]

    def block(r, c):
        return out_ref.at[:, pl.ds(pl.multiple_of((r * 4 + c) * width, width), width)]

    def move(source, r, c, slot, peer):
        return copy_to(source, block(r, c), send.at[slot], recv.at[slot], peer)

    rows = [lax.rem(row + d, 4) for d in range(4)]
    back = [lax.rem(row + 4 - d, 4) for d in range(4)]
    sent = {}
    sent[0] = move(own_ref, row, col, 0, {"wc": cross})
    for d in (1, 3, 2):
        sent[d] = move(own_ref, row, col, d, {"wr": rows[d]})
    sent[7] = move(own_ref, row, col, 7, {"wc": mate})
    sent[0].wait_recv()
    for d in (1, 3, 2):
        sent[3 + d] = move(block(row, cross), row, cross, 3 + d, {"wr": rows[d]})
    sent[8] = move(block(row, cross), row, cross, 8, {"wc": mate})
    for d in (1, 3, 2):
        sent[d].wait_recv()
        sent[8 + d] = move(block(back[d], col), back[d], col, 8 + d, {"wc": mate})
    for d in (1, 3, 2):
        sent[3 + d].wait_recv()
        sent[11 + d] = move(block(back[d], cross), back[d], cross, 11 + d, {"wc": mate})
    for slot in range(7, 15):
        sent[slot].wait_recv()
    for slot in range(15):
        sent[slot].wait_send()


def gather16(own):
    rows, width = own.shape

    def kernel(own_ref, out_ref, send, recv):
        row, col, core, cross, mate = plane()
        greet(plane_peers(row, cross, mate))
        out_ref[:, pl.ds(pl.multiple_of((row * 4 + col) * width, width), width)] = own_ref[...]
        gather_plane(own_ref, out_ref, send, recv)

    return pl.pallas_call(
        kernel,
        out_shape=jax.ShapeDtypeStruct((rows, width * 16), own.dtype),
        in_specs=[VM],
        out_specs=VM,
        scratch_shapes=[DMA((15,)), DMA((15,))],
        compiler_params=params(1),
        name="gather_tokens",
    )(own)


def gather_head(branch):
    rows, width = branch.shape
    rim = 16

    def kernel(own_ref, out_ref, rim_ref, send, recv):
        row, col, core, cross, mate = plane()
        place = lax.axis_index("seq")
        after = lax.rem(place + 1, SEQ)
        onward = [{"seq": after, "wc": lax.rem(col + j, 4)} for j in range(4)]
        before = lax.rem(place + SEQ - 1, SEQ)
        greet([{"wc": cross}, {"wc": mate}] + [{"seq": before, "wc": lax.rem(col + j, 4)} for j in range(4)])

        def block(ref, c):
            return ref.at[:, pl.ds(pl.multiple_of(c * width, width), width)]

        over = copy_to(own_ref, block(out_ref, col), send.at[0], recv.at[0], {"wc": cross})
        side = copy_to(own_ref, block(out_ref, col), send.at[1], recv.at[1], {"wc": mate})
        tails = [
            copy_to(own_ref.at[pl.ds(rows - rim, rim)], block(rim_ref, col), send.at[3 + j], recv.at[3 + j], onward[j])
            for j in range(4)
        ]
        out_ref[:, pl.ds(pl.multiple_of(col * width, width), width)] = own_ref[...]
        over.wait_recv()
        last = copy_to(block(out_ref, cross), block(out_ref, cross), send.at[2], recv.at[2], {"wc": mate})
        side.wait_recv()
        for tail in tails:
            tail.wait_recv()
        last.wait_recv()
        for made in [over, side, last] + tails:
            made.wait_send()

    return pl.pallas_call(
        kernel,
        out_shape=(
            jax.ShapeDtypeStruct((rows, width * 4), branch.dtype),
            jax.ShapeDtypeStruct((rim, width * 4), branch.dtype),
        ),
        in_specs=[VM],
        out_specs=(VM, VM),
        scratch_shapes=[DMA((7,)), DMA((7,))],
        compiler_params=params(2),
        name="gather_head",
    )(branch)


SMALL = 24


def scan_states(grown, ends_a, ends_b, small):
    spans, part, width = grown.shape

    def kernel(
        grown_ref, a_ref, b_ref, small_ref, state_ref, chosen_ref, edge_ref,
        got, got_a, got_b, got_small, going, total, send, recv, local,
    ):
        place = lax.axis_index("seq")
        peers = [lax.rem(place + d, SEQ) for d in range(SEQ)]
        greet([{"seq": peers[d]} for d in range(1, SEQ)])
        sent = [[], [], [], []]
        for d in range(1, SEQ):
            to = {"seq": peers[d]}
            sent[0].append(copy_to(small_ref, got_small.at[place], send.at[0, d], recv.at[0, d], to))
            sent[1].append(copy_to(grown_ref.at[peers[d]], got.at[place], send.at[1, d], recv.at[1, d], to))
        own = [
            pltpu.make_async_copy(small_ref, got_small.at[place], local.at[0]),
            pltpu.make_async_copy(grown_ref.at[place], got.at[place], local.at[1]),
            pltpu.make_async_copy(a_ref.at[place], got_a.at[place], local.at[2]),
        ]
        for made in own:
            made.start()
        for d in range(1, SEQ):
            to = {"seq": peers[d]}
            sent[2].append(copy_to(a_ref.at[peers[d]], got_a.at[place], send.at[2, d], recv.at[2, d], to))
        b_copies = [
            pltpu.make_async_remote_copy(
                src_ref=b_ref.at[peers[d]], dst_ref=got_b, send_sem=send.at[4, d], recv_sem=recv.at[4, 0],
                device_id={"seq": peers[d]}, device_id_type=MESH,
            )
            for d in range(1, SEQ)
        ]

        @pl.when(place == SPLIT)
        def _():
            for made in b_copies:
                made.start()
            made = pltpu.make_async_copy(b_ref.at[place], got_b, local.at[3])
            made.start()
            made.wait()

        for made in own:
            made.wait()
        for made in sent[0] + sent[1]:
            made.wait_recv()
        state = jnp.zeros((part, width), jnp.float32)
        first = jnp.zeros((part, width), jnp.float32)
        second = jnp.zeros((part, width), jnp.float32)
        for k in range(SEQ):
            going[k] = state.astype(jnp.bfloat16)
            if k <= SPLIT:
                first = first + got_small[k, 10:11] * state
            if k >= SPLIT:
                second = second + got_small[k, 11:12] * state
            state = got_small[k, 9:10] * state + got[k].astype(jnp.float32)
        total[0] = first
        total[1] = second
        total[2] = state
        for d in range(1, SEQ):
            sent[3].append(
                copy_to(going.at[peers[d]], state_ref.at[place], send.at[3, d], recv.at[3, d], {"seq": peers[d]})
            )
        state_ref[place] = going[place]
        edge = got_small[0, 0:16]
        for k in range(1, SEQ):
            edge = edge + got_small[k, 0:16]
        edge_ref[...] = edge
        for made in sent[2]:
            made.wait_recv()

        @pl.when(place != SPLIT)
        def _():
            b_copies[0].wait_recv()

        first, second, third = total[0], total[1] + got_b[...].astype(jnp.float32), total[2]
        for k in range(SEQ):
            if k <= SPLIT:
                first = first + got_a[k].astype(jnp.float32)
            else:
                second = second + got_a[k].astype(jnp.float32)
        for k in range(SEQ):
            for j in range(2):
                row = 12 + 3 * j
                chosen_ref[k, j] = (
                    got_small[k, row : row + 1] * first
                    + got_small[k, row + 1 : row + 2] * second
                    + got_small[k, row + 2 : row + 3] * third
                ).astype(jnp.bfloat16)
        for made in sent[3]:
            made.wait_recv()
        for group in sent:
            for made in group:
                made.wait_send()

        @pl.when(place == SPLIT)
        def _():
            for made in b_copies:
                made.wait_send()

    return pl.pallas_call(
        kernel,
        out_shape=(
            jax.ShapeDtypeStruct((spans, part, width), jnp.bfloat16),
            jax.ShapeDtypeStruct((spans, 2, part, width), jnp.bfloat16),
            jax.ShapeDtypeStruct((16, width), jnp.float32),
        ),
        in_specs=[VM] * 4,
        out_specs=(VM, VM, VM),
        scratch_shapes=[
            pltpu.VMEM((spans, part, width), jnp.bfloat16),
            pltpu.VMEM((spans, part, width), jnp.bfloat16),
            pltpu.VMEM((part, width), jnp.bfloat16),
            pltpu.VMEM((spans, SMALL, width), jnp.float32),
            pltpu.VMEM((spans, part, width), jnp.bfloat16),
            pltpu.VMEM((3, part, width), jnp.float32),
            DMA((5, SEQ)),
            DMA((5, SEQ)),
            DMA((4,)),
        ],
        compiler_params=params(3),
        name="scan_states",
    )(grown, ends_a, ends_b, small)


def sum_wc(sums):
    def kernel(own_ref, out_ref, got, send, recv):
        col = lax.axis_index("wc")
        peers = [{"wc": lax.rem(col + d, 4)} for d in (1, 2, 3)]
        greet(peers)
        sent = [copy_to(own_ref, got.at[d], send.at[d], recv.at[d], peers[d]) for d in range(3)]
        for made in sent:
            made.wait()
        out_ref[...] = own_ref[...] + got[0] + got[1] + got[2]

    return pl.pallas_call(
        kernel,
        out_shape=jax.ShapeDtypeStruct(sums.shape, sums.dtype),
        in_specs=[VM],
        out_specs=VM,
        scratch_shapes=[pltpu.VMEM((3,) + sums.shape, sums.dtype), DMA((3,)), DMA((3,))],
        compiler_params=params(4),
        name="sum_wc",
    )(sums)


def reduce_plane(terms, current, chosen, gather):
    rows, width = current.shape
    spans, reqs, part, cols = chosen.shape

    def kernel(*refs):
        if gather:
            (term_ref, cur_ref, chosen_ref, new_ref, req_ref, out_ref, near, held, far, last, pair,
             send, recv, fsend, frecv, local, gsend, grecv) = refs
        else:
            (term_ref, cur_ref, chosen_ref, new_ref, req_ref, near, held, far, last, pair,
             send, recv, fsend, frecv, local) = refs
        place = lax.axis_index("seq")
        row, col, core, cross, mate = plane()
        spans_to = [lax.rem(place + d, SEQ) for d in range(SEQ)]
        greet(plane_peers(row, cross, mate) + [{"seq": spans_to[d]} for d in range(1, SEQ)])
        order = [2, 1, 3, 0]
        rows_to = [lax.rem(row + d, 4) for d in range(4)]

        def block(r, c):
            return pl.ds(pl.multiple_of((r * 4 + c) * width, width), width)

        first = []
        for i, d in enumerate(order):
            for h in range(2):
                first.append(
                    copy_to(
                        term_ref.at[:, block(rows_to[d], 2 * h + 1 - core)], near.at[2 * d + h],
                        send.at[2 * d + h], recv.at[2 * d + h], {"wc": mate},
                    )
                )
        side = [
            copy_to(chosen_ref.at[spans_to[d]], req_ref.at[:, place], fsend.at[d], frecv.at[d], {"seq": spans_to[d]})
            for d in range(1, SEQ)
        ]
        keep = pltpu.make_async_copy(chosen_ref.at[place], req_ref.at[:, place], local)
        keep.start()
        second = []
        for i, d in enumerate(order):
            for h in range(2):
                first[2 * i + h].wait_recv()
                total = term_ref[:, block(rows_to[d], 2 * h + core)].astype(jnp.float32) + near[2 * d + h].astype(
                    jnp.float32
                )
                if d > 0:
                    held[2 * d + h] = total.astype(jnp.bfloat16)
                else:
                    pair[h] = total
            if d > 0:
                second.append(
                    copy_to(
                        held.at[pl.ds(2 * d, 2)], far.at[d - 1], send.at[8 + d], recv.at[8 + d], {"wr": rows_to[d]}
                    )
                )
        for made in second:
            made.wait_recv()
        other = lax.rem(lax.div(col, 2) + 1, 2)
        for h in range(2):
            pair[h] = (
                pair[h]
                + far[0, h].astype(jnp.float32)
                + far[1, h].astype(jnp.float32)
                + far[2, h].astype(jnp.float32)
            )
        held[0] = pair[other].astype(jnp.bfloat16)
        third = copy_to(held.at[0], last, send.at[8], recv.at[8], {"wc": cross})
        third.wait_recv()
        new_ref[...] = (
            cur_ref[...].astype(jnp.float32) + (pair[1 - other] + last[...].astype(jnp.float32))
        ).astype(jnp.bfloat16)
        if gather:
            out_ref[:, block(row, col)] = new_ref[...]
            gather_plane(new_ref, out_ref, gsend, grecv)
        for made in side:
            made.wait_recv()
        keep.wait()
        for made in first + second + [third] + side:
            made.wait_send()

    shapes = [
        jax.ShapeDtypeStruct((rows, width), jnp.bfloat16),
        jax.ShapeDtypeStruct((reqs, spans, part, cols), jnp.bfloat16),
    ]
    scratch = [
        pltpu.VMEM((8, rows, width), jnp.bfloat16),
        pltpu.VMEM((8, rows, width), jnp.bfloat16),
        pltpu.VMEM((3, 2, rows, width), jnp.bfloat16),
        pltpu.VMEM((rows, width), jnp.bfloat16),
        pltpu.VMEM((2, rows, width), jnp.float32),
        DMA((12,)), DMA((12,)), DMA((SEQ,)), DMA((SEQ,)), DMA,
    ]
    if gather:
        shapes.append(jax.ShapeDtypeStruct((rows, width * 16), jnp.bfloat16))
        scratch += [DMA((15,)), DMA((15,))]
    return pl.pallas_call(
        kernel,
        out_shape=tuple(shapes),
        in_specs=[VM] * 3,
        out_specs=(VM,) * len(shapes),
        scratch_shapes=scratch,
        compiler_params=params(5 if gather else 6),
        name="reduce_gather" if gather else "reduce_last",
    )(terms, current, chosen)


def norm_rows(source, gain_row):
    widened = source.astype(jnp.float32)
    row_mean = jnp.mean(widened, axis=1, keepdims=True)
    row_var = jnp.mean(widened * widened, axis=1, keepdims=True) - row_mean * row_mean
    return ((widened - row_mean) * lax.rsqrt(row_var + EPSILON) * gain_row).astype(jnp.bfloat16)


def segment_of(positions, lengths):
    bound_one = lengths[0]
    bound_two = lengths[0] + lengths[1]
    return (positions >= bound_one).astype(jnp.int32) + (positions >= bound_two).astype(jnp.int32)


def conv_rows(extended, ext_segment, segment, weight, bias_row):
    row_count = segment.shape[0]
    widened = extended.astype(jnp.float32)
    summed = jnp.zeros((row_count, widened.shape[1]), jnp.float32) + bias_row
    for back_step in range(weight.shape[0]):
        low_row = weight.shape[0] - 1 - back_step
        keep_row = (ext_segment[low_row : low_row + row_count] == segment).astype(jnp.float32)
        summed = (
            summed + weight[back_step] * widened[low_row : low_row + row_count] * keep_row[:, None]
        )
    return jax.nn.silu(summed).astype(jnp.bfloat16)


def block_mix(source, weight):
    group = weight.shape[2]
    widened = source.astype(jnp.float32)
    blocks = [
        sum(widened[:, i * group : (i + 1) * group] * weight[i, j] for i in range(4))
        for j in range(weight.shape[1])
    ]
    return jnp.concatenate(blocks, axis=1) if len(blocks) > 1 else blocks[0]


def body(
    tokens, ln_gain, w_branch, w_outgate, w_gates, forget_bias, conv_weight, conv_bias, w_query, w_key, w_value,
    skip_gain, norm_gain, w_down, lengths, request_prompt,
):
    tok_rows = tokens.shape[0]
    seq_index = lax.axis_index("seq")
    head_idx = lax.axis_index("wr")
    col_idx = lax.axis_index("wc")
    row_offset = seq_index * tok_rows
    total_rows = tok_rows * SEQ
    positions = row_offset + jnp.arange(tok_rows, dtype=jnp.int32)
    segment = segment_of(positions, lengths)
    seg_before = jnp.where(row_offset > 0, segment_of(row_offset - 1, lengths), -1)
    rim_positions = row_offset - (CONV - 1) + jnp.arange(CONV - 1, dtype=jnp.int32)
    rim_segment = jnp.where(rim_positions >= 0, segment_of(rim_positions, lengths), -1)
    ext_segment = jnp.concatenate([rim_segment, segment])
    starts = [jnp.zeros((), jnp.int32), lengths[0], lengths[0] + lengths[1]]
    ends = [lengths[0] - 1, lengths[0] + lengths[1] - 1, jnp.zeros((), jnp.int32) + (total_rows - 1)]
    holders = [(end >= row_offset) & (end < row_offset + tok_rows) for end in ends]
    local_ends = [jnp.clip(end - row_offset, 0, tok_rows - 1) for end in ends]
    head_mask = (jnp.arange(HEADS, dtype=jnp.int32) == head_idx).astype(jnp.float32)
    row_order = jnp.arange(tok_rows)
    allowed = (row_order[:, None] >= row_order[None, :]) & (segment[:, None] == segment[None, :])
    choice = (request_prompt[:, None] == jnp.arange(PROMPTS, dtype=jnp.int32)[None, :]).astype(jnp.float32)
    conv_all = jnp.concatenate([conv_weight, conv_bias[:, None]], axis=1)
    conv_all = lax.all_gather(conv_all, "wc", axis=2, tiled=True)
    current = tokens
    gathered = gather16(tokens)
    states = []
    edges_out = []
    for layer in range(LAYERS):
        normed = norm_rows(gathered, ln_gain[layer])
        branch = jnp.dot(normed, w_branch[layer], preferred_element_type=jnp.float32).astype(jnp.bfloat16)
        outgate = jnp.dot(normed, w_outgate[layer], preferred_element_type=jnp.float32)
        gate_pre = jnp.dot(normed, w_gates[layer], preferred_element_type=jnp.float32)
        input_pre = jnp.sum(gate_pre[:, :HEADS] * head_mask, axis=1)
        forget_pre = jnp.sum((gate_pre[:, HEADS:] + forget_bias[layer]) * head_mask, axis=1)
        in_gate = GATE_CAP * jnp.tanh(input_pre / GATE_CAP)
        log_forget = jax.nn.log_sigmoid(forget_pre)
        head_branch, rim = gather_head(branch)
        width = branch.shape[1]
        extended = jnp.concatenate([rim[rim.shape[0] - (CONV - 1) :], head_branch], axis=0)
        head_act = conv_rows(extended, ext_segment, segment, conv_all[layer, :CONV], conv_all[layer, CONV])
        head_width = head_act.shape[1]
        queries = block_mix(head_act, w_query[layer, 0]).astype(jnp.bfloat16)
        key_rows = (block_mix(head_act, w_key[layer, 0]) * head_width ** (-0.5)).astype(jnp.bfloat16)
        values = block_mix(head_branch, w_value[layer, 0]).astype(jnp.bfloat16)
        cum_log = jnp.cumsum(log_forget)
        end_cum = cum_log[tok_rows - 1]
        last_seg = segment[tok_rows - 1]
        grow = jnp.where(segment == last_seg, jnp.exp(end_cum - cum_log + in_gate), 0.0)
        decay = jnp.where(last_seg == seg_before, jnp.exp(end_cum), 0.0)
        end_weights = []
        end_decays = []
        for prompt in range(2):
            local_cum = cum_log[local_ends[prompt]]
            chosen = holders[prompt] & (segment == prompt) & (row_order <= local_ends[prompt])
            end_weights.append(jnp.exp(jnp.where(chosen, local_cum - cum_log + in_gate, -jnp.inf)))
            end_decays.append(jnp.where(holders[prompt] & (seg_before == prompt), jnp.exp(local_cum), 0.0))
        weight_a = jnp.where(seq_index <= SPLIT, end_weights[0], end_weights[1])
        weights = jnp.stack([grow, weight_a, end_weights[1]], axis=1)
        weighted = (values.astype(jnp.float32)[:, None, :] * weights[:, :, None]).astype(jnp.bfloat16)
        sums = lax.dot_general(
            key_rows, weighted.reshape(tok_rows, -1), ROW_DIMS, preferred_element_type=jnp.float32
        ).astype(jnp.bfloat16)
        sums = sums.reshape(SEQ, head_width // SEQ, 3, width)
        own_extended = lax.dynamic_slice_in_dim(extended, col_idx * width, width, 1)
        small_rows = []
        for prompt in range(PROMPTS):
            window = lax.dynamic_slice_in_dim(own_extended, local_ends[prompt] + 1, CONV - 1, 0)
            edge_pos = ends[prompt] - (CONV - 2) + jnp.arange(CONV - 1, dtype=jnp.int32)
            keep = (edge_pos >= starts[prompt]) & holders[prompt]
            small_rows.append(jnp.where(keep[:, None], window.astype(jnp.float32), 0.0))
        scalars = jnp.concatenate([jnp.stack([decay] + end_decays), choice.reshape(-1), jnp.zeros((SMALL - 18,))])
        small = jnp.concatenate(small_rows + [jnp.broadcast_to(scalars[:, None], (scalars.shape[0], width))], axis=0)
        scores = lax.dot_general(queries, key_rows, FEATURE_DIMS, preferred_element_type=jnp.float32) * jnp.exp(
            jnp.where(allowed, cum_log[:, None] - cum_log[None, :] + in_gate[None, :], -jnp.inf)
        )
        in_block = jnp.dot(scores.astype(jnp.bfloat16), values, preferred_element_type=jnp.float32)
        carried = jnp.where(segment == seg_before, jnp.exp(cum_log), 0.0)
        state, chosen_states, edge_sum = scan_states(sums[:, :, 0], sums[:, :, 1], sums[:, :, 2], small)
        state_here = state.reshape(head_width, width)
        hidden = in_block + carried[:, None] * jnp.dot(queries, state_here, preferred_element_type=jnp.float32)
        stats = jnp.stack([jnp.sum(hidden, axis=1), jnp.sum(hidden * hidden, axis=1)])
        stats = sum_wc(jnp.concatenate([stats, jnp.zeros((6, tok_rows), jnp.float32)]))
        row_mean = stats[0] / head_width
        row_var = stats[1] / head_width - row_mean * row_mean
        normal_rows = (hidden - row_mean[:, None]) * lax.rsqrt(row_var + EPSILON)[:, None]
        conv_act = lax.dynamic_slice_in_dim(head_act, col_idx * width, width, 1)
        gated = (
            (normal_rows * norm_gain[layer] + skip_gain[layer] * conv_act.astype(jnp.float32))
            * jax.nn.silu(outgate)
        ).astype(jnp.bfloat16)
        terms = jnp.dot(gated, w_down[layer], preferred_element_type=jnp.float32).astype(jnp.bfloat16)
        made = reduce_plane(terms, current, chosen_states, layer + 1 < LAYERS)
        current = made[0]
        states.append(made[1].reshape(2, 1, head_width, width))
        if layer + 1 < LAYERS:
            gathered = made[2]
        edges_out.append(
            jnp.einsum(
                "rp,pkc->rkc", choice, edge_sum[:9].reshape(PROMPTS, CONV - 1, width), precision=lax.Precision.HIGHEST
            ).astype(jnp.bfloat16)
        )
    return (current, jnp.stack(states), jnp.stack(edges_out))


def solution(mesh):
    return jax.shard_map(
        body,
        mesh=mesh,
        in_specs=(
            P("seq", ("wr", "wc")),
            P(),
            P(None, None, ("wr", "wc")),
            P(None, None, ("wr", "wc")),
            P(),
            P(),
            P(None, None, ("wr", "wc")),
            P(None, ("wr", "wc")),
            P(None, "wr", None, None, None),
            P(None, "wr", None, None, None),
            P(None, "wr", None, "wc", None),
            P(None, ("wr", "wc")),
            P(None, ("wr", "wc")),
            P(None, ("wr", "wc"), None),
            P(),
            P("seq"),
        ),
        out_specs=(
            P("seq", ("wr", "wc")),
            P(None, "seq", "wr", None, "wc"),
            P(None, "seq", None, ("wr", "wc")),
        ),
        check_vma=False,
    )
```

```python
import jax
import jax.numpy as jnp
from jax import lax
from jax.experimental import pallas as pl
from jax.experimental.pallas import tpu as pltpu
from jax.sharding import PartitionSpec as P

HEADS = 4
CONV = 4
LAYERS = 2
PROMPTS = 3
SEQ = 16
SPLIT = 7

EPSILON = 1e-05
GATE_CAP = 15.0
FEATURE_DIMS = (((1,), (1,)), ((), ()))
ROW_DIMS = (((0,), (0,)), ((), ()))
MESH = pl.DeviceIdType.MESH
VM = pl.BlockSpec(memory_space=pltpu.VMEM)
DMA = pltpu.SemaphoreType.DMA


def params(collective):
    return pltpu.CompilerParams(
        collective_id=collective, has_side_effects=True, vmem_limit_bytes=48 * 1024 * 1024
    )


def greet(peers):
    barrier = pltpu.get_barrier_semaphore()
    for peer in peers:
        pl.semaphore_signal(barrier, inc=1, device_id=peer, device_id_type=MESH)
    pl.semaphore_wait(barrier, len(peers))


def copy_to(source, target, send, recv, peer):
    made = pltpu.make_async_remote_copy(
        src_ref=source, dst_ref=target, send_sem=send, recv_sem=recv, device_id=peer, device_id_type=MESH
    )
    made.start()
    return made


def plane():
    row, col = lax.axis_index("wr"), lax.axis_index("wc")
    core = lax.rem(col, 2)
    cross = lax.rem(col + 2, 4)
    mate = col + 1 - 2 * core
    return row, col, core, cross, mate


def plane_peers(row, cross, mate):
    return [{"wr": lax.rem(row + d, 4)} for d in (1, 2, 3)] + [{"wc": cross}, {"wc": mate}]


def gather_plane(own_ref, out_ref, send, recv):
    row, col, core, cross, mate = plane()
    mate_cross = lax.rem(mate + 2, 4)
    width = own_ref.shape[1]

    def block(r, c):
        return out_ref.at[:, pl.ds(pl.multiple_of((r * 4 + c) * width, width), width)]

    def move(source, r, c, slot, peer):
        return copy_to(source, block(r, c), send.at[slot], recv.at[slot], peer)

    rows = [lax.rem(row + d, 4) for d in range(4)]
    back = [lax.rem(row + 4 - d, 4) for d in range(4)]
    sent = {}
    sent[0] = move(own_ref, row, col, 0, {"wc": cross})
    for d in (1, 3, 2):
        sent[d] = move(own_ref, row, col, d, {"wr": rows[d]})
    sent[7] = move(own_ref, row, col, 7, {"wc": mate})
    sent[0].wait_recv()
    for d in (1, 3, 2):
        sent[3 + d] = move(block(row, cross), row, cross, 3 + d, {"wr": rows[d]})
    sent[8] = move(block(row, cross), row, cross, 8, {"wc": mate})
    for d in (1, 3, 2):
        sent[d].wait_recv()
        sent[8 + d] = move(block(back[d], col), back[d], col, 8 + d, {"wc": mate})
    for d in (1, 3, 2):
        sent[3 + d].wait_recv()
        sent[11 + d] = move(block(back[d], cross), back[d], cross, 11 + d, {"wc": mate})
    for slot in range(7, 15):
        sent[slot].wait_recv()
    for slot in range(15):
        sent[slot].wait_send()


def gather16(own):
    rows, width = own.shape

    def kernel(own_ref, out_ref, send, recv):
        row, col, core, cross, mate = plane()
        greet(plane_peers(row, cross, mate))
        out_ref[:, pl.ds(pl.multiple_of((row * 4 + col) * width, width), width)] = own_ref[...]
        gather_plane(own_ref, out_ref, send, recv)

    return pl.pallas_call(
        kernel,
        out_shape=jax.ShapeDtypeStruct((rows, width * 16), own.dtype),
        in_specs=[VM],
        out_specs=VM,
        scratch_shapes=[DMA((15,)), DMA((15,))],
        compiler_params=params(1),
        name="gather_tokens",
    )(own)


def gather_head(branch):
    rows, width = branch.shape
    rim = 16

    def kernel(own_ref, out_ref, rim_ref, send, recv):
        row, col, core, cross, mate = plane()
        place = lax.axis_index("seq")
        after = lax.rem(place + 1, SEQ)
        onward = [{"seq": after, "wc": lax.rem(col + j, 4)} for j in range(4)]
        before = lax.rem(place + SEQ - 1, SEQ)
        greet([{"wc": cross}, {"wc": mate}] + [{"seq": before, "wc": lax.rem(col + j, 4)} for j in range(4)])

        def block(ref, c):
            return ref.at[:, pl.ds(pl.multiple_of(c * width, width), width)]

        over = copy_to(own_ref, block(out_ref, col), send.at[0], recv.at[0], {"wc": cross})
        side = copy_to(own_ref, block(out_ref, col), send.at[1], recv.at[1], {"wc": mate})
        tails = [
            copy_to(own_ref.at[pl.ds(rows - rim, rim)], block(rim_ref, col), send.at[3 + j], recv.at[3 + j], onward[j])
            for j in range(4)
        ]
        out_ref[:, pl.ds(pl.multiple_of(col * width, width), width)] = own_ref[...]
        over.wait_recv()
        last = copy_to(block(out_ref, cross), block(out_ref, cross), send.at[2], recv.at[2], {"wc": mate})
        side.wait_recv()
        for tail in tails:
            tail.wait_recv()
        last.wait_recv()
        for made in [over, side, last] + tails:
            made.wait_send()

    return pl.pallas_call(
        kernel,
        out_shape=(
            jax.ShapeDtypeStruct((rows, width * 4), branch.dtype),
            jax.ShapeDtypeStruct((rim, width * 4), branch.dtype),
        ),
        in_specs=[VM],
        out_specs=(VM, VM),
        scratch_shapes=[DMA((7,)), DMA((7,))],
        compiler_params=params(2),
        name="gather_head",
    )(branch)


def tail(sums, small, edges, lines, queries, keys, values, act, outgate, gains, w_down, current, gather):
    spans, part, wide = sums.shape
    cols = wide // 3
    rows, width = current.shape
    head_width = queries.shape[1]
    tile = 128
    tiles = rows // tile

    def kernel(
        sums_ref, small_ref, edges_ref, lines_ref, q_ref, k_ref, v_ref, act_ref, og_ref, gains_ref, down_ref, cur_ref,
        *refs,
    ):
        new_ref, req_ref, edge_ref = refs[:3]
        if gather:
            out_ref, gsend, grecv = refs[3], refs[-2], refs[-1]
            refs = refs[:3] + refs[4:-2]
        (got, got_a, got_b, got_small, got_edges, going, state_ref, total, chosen, upright, hidden, stat, got_stat,
         gated, term, near, held, far, last, pair, send, recv, esend, erecv, local) = refs[3:]
        place = lax.axis_index("seq")
        row, col, core, cross, mate = plane()
        peers = [lax.rem(place + d, SEQ) for d in range(SEQ)]
        wc_peers = [{"wc": lax.rem(col + d, 4)} for d in (1, 2, 3)]
        greet(
            [{"wr": lax.rem(row + d, 4)} for d in (1, 2, 3)] + wc_peers + [{"seq": peers[d]} for d in range(1, SEQ)]
        )
        inc, end_a, end_b = [pl.ds(i * cols, cols) for i in range(3)]
        sent = []
        arrive = []
        for d in range(1, SEQ):
            to = {"seq": peers[d]}
            arrive.append(copy_to(small_ref, got_small.at[place], send.at[0, d], recv.at[0, d], to))
            arrive.append(copy_to(sums_ref.at[peers[d], :, inc], got.at[place], send.at[1, d], recv.at[1, d], to))
        sent += arrive
        own = [
            pltpu.make_async_copy(small_ref, got_small.at[place], local.at[0]),
            pltpu.make_async_copy(sums_ref.at[place, :, inc], got.at[place], local.at[1]),
            pltpu.make_async_copy(sums_ref.at[place, :, end_a], got_a.at[place], local.at[2]),
            pltpu.make_async_copy(edges_ref, got_edges.at[place], local.at[3]),
        ]
        for made in own:
            made.start()

        upright[...] = jnp.transpose(
            jnp.concatenate([lines_ref[...], jnp.zeros((128 - lines_ref.shape[0], rows), jnp.float32)])
        )
        for r in range(tiles):
            at = pl.ds(r * tile, tile)
            seen = (r + 1) * tile
            scores = lax.dot_general(
                q_ref[at], k_ref[pl.ds(0, seen)], FEATURE_DIMS, preferred_element_type=jnp.float32
            )
            gap = upright[at, 0:1] - lines_ref[0:1, 0:seen] + lines_ref[1:2, 0:seen]
            early = (
                lax.broadcasted_iota(jnp.int32, (tile, seen), 0) + r * tile
                >= lax.broadcasted_iota(jnp.int32, (tile, seen), 1)
            )
            allowed = early & (upright[at, 2:3] == lines_ref[2:3, 0:seen])
            scores = scores * jnp.exp(jnp.where(allowed, gap, -jnp.inf))
            hidden[at] = jnp.dot(
                scores.astype(jnp.bfloat16), v_ref[pl.ds(0, seen)], preferred_element_type=jnp.float32
            )

        for made in own:
            made.wait()
        for made in arrive:
            made.wait_recv()

        def scalar(k, i):
            line = got_small[k, i : i + 1]
            return jnp.concatenate([line] * (cols // 128), axis=1)

        state = jnp.zeros((part, cols), jnp.float32)
        first = jnp.zeros((part, cols), jnp.float32)
        second = jnp.zeros((part, cols), jnp.float32)
        for k in range(SEQ):
            going[k] = state.astype(jnp.bfloat16)
            if k <= SPLIT:
                first = first + scalar(k, 1) * state
            if k >= SPLIT:
                second = second + scalar(k, 2) * state
            state = scalar(k, 0) * state + got[k].astype(jnp.float32)
        total[0] = first
        total[1] = second
        total[2] = state
        arrive = [
            copy_to(going.at[peers[d]], state_ref.at[place], send.at[3, d], recv.at[3, d], {"seq": peers[d]})
            for d in range(1, SEQ)
        ]
        sent += arrive
        state_ref[place] = going[place]
        for made in arrive:
            made.wait_recv()
        late = []
        for d in range(1, SEQ):
            to = {"seq": peers[d]}
            late.append(copy_to(edges_ref, got_edges.at[place], send.at[5, d], recv.at[5, d], to))
            late.append(copy_to(sums_ref.at[peers[d], :, end_a], got_a.at[place], send.at[2, d], recv.at[2, d], to))
        sent += late
        b_copies = [
            pltpu.make_async_remote_copy(
                src_ref=sums_ref.at[peers[d], :, end_b], dst_ref=got_b, send_sem=send.at[4, d], recv_sem=recv.at[4, 0],
                device_id={"seq": peers[d]}, device_id_type=MESH,
            )
            for d in range(1, SEQ)
        ]

        @pl.when(place == SPLIT)
        def _():
            for made in b_copies:
                made.start()
            made = pltpu.make_async_copy(sums_ref.at[place, :, end_b], got_b, local.at[4])
            made.start()
            made.wait()

        lane = lax.broadcasted_iota(jnp.int32, (tile, 128), 1)
        whole = state_ref[...].reshape(head_width, cols)
        for r in range(tiles):
            at = pl.ds(r * tile, tile)
            here = hidden[at] + upright[at, 3:4] * jnp.dot(q_ref[at], whole, preferred_element_type=jnp.float32)
            hidden[at] = here
            ones = jnp.sum(here, axis=1, keepdims=True)
            twos = jnp.sum(here * here, axis=1, keepdims=True)
            upright[at] = jnp.where(lane == 0, ones, jnp.where(lane == 1, twos, 0.0))
        stat[...] = jnp.transpose(upright[...])[0:8]
        arrive = [copy_to(stat, got_stat.at[d], esend.at[d], erecv.at[d], wc_peers[d]) for d in range(3)]
        sent += arrive
        for made in arrive:
            made.wait_recv()
        sums_all = stat[...] + got_stat[0] + got_stat[1] + got_stat[2]
        upright[...] = jnp.transpose(jnp.concatenate([sums_all, jnp.zeros((120, rows), jnp.float32)]))
        for r in range(tiles):
            at = pl.ds(r * tile, tile)
            mean = upright[at, 0:1] / head_width
            var = upright[at, 1:2] / head_width - mean * mean
            normal = (hidden[at] - mean) * lax.rsqrt(var + EPSILON)
            gate = og_ref[at]
            gated[at] = (
                (normal * gains_ref[0:1] + gains_ref[1:2] * act_ref[at].astype(jnp.float32)) * (gate * jax.nn.sigmoid(gate))
            ).astype(jnp.bfloat16)

        order = [2, 1, 3, 0]
        rows_to = [lax.rem(row + d, 4) for d in range(4)]
        first = []
        for d in order:
            term[d] = jnp.dot(
                gated[...], down_ref[:, pl.ds(pl.multiple_of(rows_to[d] * 4 * width, 4 * width), 4 * width)],
                preferred_element_type=jnp.float32,
            ).astype(jnp.bfloat16)
            for h in range(2):
                first.append(
                    copy_to(
                        term.at[d, :, pl.ds(pl.multiple_of((2 * h + 1 - core) * width, width), width)],
                        near.at[2 * d + h], send.at[6, 2 * d + h], recv.at[6, 2 * d + h], {"wc": mate},
                    )
                )
        second = []
        for i, d in enumerate(order):
            for h in range(2):
                first[2 * i + h].wait_recv()
                block = term[d, :, pl.ds(pl.multiple_of((2 * h + core) * width, width), width)]
                whole = block.astype(jnp.float32) + near[2 * d + h].astype(jnp.float32)
                if d > 0:
                    held[2 * d + h] = whole.astype(jnp.bfloat16)
                else:
                    pair[h] = whole
            if d > 0:
                second.append(
                    copy_to(held.at[pl.ds(2 * d, 2)], far.at[d - 1], esend.at[4 + d], erecv.at[4 + d], {"wr": rows_to[d]})
                )
        sent += first + second

        for made in late:
            made.wait_recv()

        @pl.when(place != SPLIT)
        def _():
            b_copies[0].wait_recv()

        first, second_end, third = total[0], total[1] + got_b[...].astype(jnp.float32), total[2]
        edge = jnp.zeros((16, cols), jnp.float32)
        for k in range(SEQ):
            edge = edge + got_edges[k].astype(jnp.float32)
            if k <= SPLIT:
                first = first + got_a[k].astype(jnp.float32)
            else:
                second_end = second_end + got_a[k].astype(jnp.float32)
        total[0] = first
        total[1] = second_end
        side = []
        for d in range(1, SEQ):
            for j in range(2):
                which = got_small[peers[d], 3 + j : 4 + j]
                which = jnp.concatenate([which] * (cols // 128), axis=1)
                chosen[peers[d], j] = jnp.where(
                    which == 0.0, total[0], jnp.where(which == 1.0, total[1], total[2])
                ).astype(jnp.bfloat16)
            side.append(
                copy_to(chosen.at[peers[d]], req_ref.at[:, place], send.at[7, d], recv.at[7, d], {"seq": peers[d]})
            )
        for j in range(2):
            which = small_ref[3 + j : 4 + j]
            which = jnp.concatenate([which] * (cols // 128), axis=1)
            req_ref[j, place] = jnp.where(
                which == 0.0, total[0], jnp.where(which == 1.0, total[1], total[2])
            ).astype(jnp.bfloat16)
            edge_ref[j, 0:3] = jnp.where(
                which == 0.0, edge[0:3], jnp.where(which == 1.0, edge[3:6], edge[6:9])
            )
        sent += side

        for made in second:
            made.wait_recv()
        other = lax.rem(lax.div(col, 2) + 1, 2)
        for h in range(2):
            pair[h] = (
                pair[h]
                + far[0, h].astype(jnp.float32)
                + far[1, h].astype(jnp.float32)
                + far[2, h].astype(jnp.float32)
            )
        held[0] = pair[other].astype(jnp.bfloat16)
        final = copy_to(held.at[0], last, esend.at[4], erecv.at[4], {"wc": cross})
        sent.append(final)
        final.wait_recv()
        new_ref[...] = (
            cur_ref[...].astype(jnp.float32) + (pair[1 - other] + last[...].astype(jnp.float32))
        ).astype(jnp.bfloat16)
        if gather:
            out_ref[:, pl.ds(pl.multiple_of((row * 4 + col) * width, width), width)] = new_ref[...]
            gather_plane(new_ref, out_ref, gsend, grecv)
        for made in side:
            made.wait_recv()
        for made in sent:
            made.wait_send()

        @pl.when(place == SPLIT)
        def _():
            for made in b_copies:
                made.wait_send()

    b16, f32 = jnp.bfloat16, jnp.float32
    shapes = [
        jax.ShapeDtypeStruct((rows, width), b16),
        jax.ShapeDtypeStruct((2, spans, part, cols), b16),
        jax.ShapeDtypeStruct((2, 8, cols), f32),
    ]
    scratch = [
        pltpu.VMEM((spans, part, cols), b16),
        pltpu.VMEM((spans, part, cols), b16),
        pltpu.VMEM((part, cols), b16),
        pltpu.VMEM((spans, 8, 128), f32),
        pltpu.VMEM((spans, 16, cols), b16),
        pltpu.VMEM((spans, part, cols), b16),
        pltpu.VMEM((spans, part, cols), b16),
        pltpu.VMEM((3, part, cols), f32),
        pltpu.VMEM((spans, 2, part, cols), b16),
        pltpu.VMEM((rows, 128), f32),
        pltpu.VMEM((rows, cols), f32),
        pltpu.VMEM((8, rows), f32),
        pltpu.VMEM((3, 8, rows), f32),
        pltpu.VMEM((rows, cols), b16),
        pltpu.VMEM((4, rows, 4 * width), b16),
        pltpu.VMEM((8, rows, width), b16),
        pltpu.VMEM((8, rows, width), b16),
        pltpu.VMEM((3, 2, rows, width), b16),
        pltpu.VMEM((rows, width), b16),
        pltpu.VMEM((2, rows, width), f32),
        DMA((8, SEQ)), DMA((8, SEQ)), DMA((8,)), DMA((8,)), DMA((5,)),
    ]
    if gather:
        shapes.append(jax.ShapeDtypeStruct((rows, width * 16), b16))
        scratch += [DMA((15,)), DMA((15,))]
    return pl.pallas_call(
        kernel,
        out_shape=tuple(shapes),
        in_specs=[VM] * 12,
        out_specs=(VM,) * len(shapes),
        scratch_shapes=scratch,
        compiler_params=params(5 if gather else 6),
        name="tail_gather" if gather else "tail_last",
    )(sums, small, edges, lines, queries, keys, values, act, outgate, gains, w_down, current)


def norm_rows(source, gain_row):
    widened = source.astype(jnp.float32)
    row_mean = jnp.mean(widened, axis=1, keepdims=True)
    row_var = jnp.mean(widened * widened, axis=1, keepdims=True) - row_mean * row_mean
    return ((widened - row_mean) * lax.rsqrt(row_var + EPSILON) * gain_row).astype(jnp.bfloat16)


def segment_of(positions, lengths):
    bound_one = lengths[0]
    bound_two = lengths[0] + lengths[1]
    return (positions >= bound_one).astype(jnp.int32) + (positions >= bound_two).astype(jnp.int32)


def conv_rows(extended, ext_segment, segment, weight, bias_row):
    row_count = segment.shape[0]
    widened = extended.astype(jnp.float32)
    summed = jnp.zeros((row_count, widened.shape[1]), jnp.float32) + bias_row
    for back_step in range(weight.shape[0]):
        low_row = weight.shape[0] - 1 - back_step
        keep_row = (ext_segment[low_row : low_row + row_count] == segment).astype(jnp.float32)
        summed = (
            summed + weight[back_step] * widened[low_row : low_row + row_count] * keep_row[:, None]
        )
    return jax.nn.silu(summed).astype(jnp.bfloat16)


def block_mix(source, weight):
    group = weight.shape[2]
    widened = source.astype(jnp.float32)
    blocks = [
        sum(widened[:, i * group : (i + 1) * group] * weight[i, j] for i in range(4))
        for j in range(weight.shape[1])
    ]
    return jnp.concatenate(blocks, axis=1) if len(blocks) > 1 else blocks[0]


def body(
    tokens, ln_gain, w_branch, w_outgate, w_gates, forget_bias, conv_weight, conv_bias, w_query, w_key, w_value,
    skip_gain, norm_gain, w_down, lengths, request_prompt,
):
    tok_rows = tokens.shape[0]
    seq_index = lax.axis_index("seq")
    head_idx = lax.axis_index("wr")
    col_idx = lax.axis_index("wc")
    row_offset = seq_index * tok_rows
    total_rows = tok_rows * SEQ
    positions = row_offset + jnp.arange(tok_rows, dtype=jnp.int32)
    segment = segment_of(positions, lengths)
    seg_before = jnp.where(row_offset > 0, segment_of(row_offset - 1, lengths), -1)
    rim_positions = row_offset - (CONV - 1) + jnp.arange(CONV - 1, dtype=jnp.int32)
    rim_segment = jnp.where(rim_positions >= 0, segment_of(rim_positions, lengths), -1)
    ext_segment = jnp.concatenate([rim_segment, segment])
    starts = [jnp.zeros((), jnp.int32), lengths[0], lengths[0] + lengths[1]]
    ends = [lengths[0] - 1, lengths[0] + lengths[1] - 1, jnp.zeros((), jnp.int32) + (total_rows - 1)]
    holders = [(end >= row_offset) & (end < row_offset + tok_rows) for end in ends]
    local_ends = [jnp.clip(end - row_offset, 0, tok_rows - 1) for end in ends]
    head_mask = (jnp.arange(HEADS, dtype=jnp.int32) == head_idx).astype(jnp.float32)
    row_order = jnp.arange(tok_rows)
    conv_all = jnp.concatenate([conv_weight, conv_bias[:, None]], axis=1)
    conv_all = lax.all_gather(conv_all, "wc", axis=2, tiled=True)
    current = tokens
    gathered = gather16(tokens)
    states = []
    edges_out = []
    for layer in range(LAYERS):
        normed = norm_rows(gathered, ln_gain[layer])
        branch = jnp.dot(normed, w_branch[layer], preferred_element_type=jnp.float32).astype(jnp.bfloat16)
        outgate = jnp.dot(normed, w_outgate[layer], preferred_element_type=jnp.float32)
        gate_pre = jnp.dot(normed, w_gates[layer], preferred_element_type=jnp.float32)
        input_pre = jnp.sum(gate_pre[:, :HEADS] * head_mask, axis=1)
        forget_pre = jnp.sum((gate_pre[:, HEADS:] + forget_bias[layer]) * head_mask, axis=1)
        in_gate = GATE_CAP * jnp.tanh(input_pre / GATE_CAP)
        log_forget = jax.nn.log_sigmoid(forget_pre)
        head_branch, rim = gather_head(branch)
        width = branch.shape[1]
        extended = jnp.concatenate([rim[rim.shape[0] - (CONV - 1) :], head_branch], axis=0)
        head_act = conv_rows(extended, ext_segment, segment, conv_all[layer, :CONV], conv_all[layer, CONV])
        head_width = head_act.shape[1]
        queries = block_mix(head_act, w_query[layer, 0]).astype(jnp.bfloat16)
        key_rows = (block_mix(head_act, w_key[layer, 0]) * head_width ** (-0.5)).astype(jnp.bfloat16)
        values = block_mix(head_branch, w_value[layer, 0]).astype(jnp.bfloat16)
        cum_log = jnp.cumsum(log_forget)
        end_cum = cum_log[tok_rows - 1]
        last_seg = segment[tok_rows - 1]
        grow = jnp.where(segment == last_seg, jnp.exp(end_cum - cum_log + in_gate), 0.0)
        decay = jnp.where(last_seg == seg_before, jnp.exp(end_cum), 0.0)
        end_weights = []
        end_decays = []
        for prompt in range(2):
            local_cum = cum_log[local_ends[prompt]]
            chosen = holders[prompt] & (segment == prompt) & (row_order <= local_ends[prompt])
            end_weights.append(jnp.exp(jnp.where(chosen, local_cum - cum_log + in_gate, -jnp.inf)))
            end_decays.append(jnp.where(holders[prompt] & (seg_before == prompt), jnp.exp(local_cum), 0.0))
        weight_a = jnp.where(seq_index <= SPLIT, end_weights[0], end_weights[1])
        weights = jnp.stack([grow, weight_a, end_weights[1]], axis=1)
        weighted = (values.astype(jnp.float32)[:, None, :] * weights[:, :, None]).astype(jnp.bfloat16)
        sums = lax.dot_general(
            key_rows, weighted.reshape(tok_rows, -1), ROW_DIMS, preferred_element_type=jnp.float32
        ).astype(jnp.bfloat16)
        sums = sums.reshape(SEQ, head_width // SEQ, 3 * width)
        own_extended = lax.dynamic_slice_in_dim(extended, col_idx * width, width, 1)
        edge_rows = []
        for prompt in range(PROMPTS):
            window = lax.dynamic_slice_in_dim(own_extended, local_ends[prompt] + 1, CONV - 1, 0)
            edge_pos = ends[prompt] - (CONV - 2) + jnp.arange(CONV - 1, dtype=jnp.int32)
            keep = (edge_pos >= starts[prompt]) & holders[prompt]
            edge_rows.append(jnp.where(keep[:, None], window, jnp.zeros_like(window)))
        edges = jnp.concatenate(edge_rows + [jnp.zeros((7, width), jnp.bfloat16)], axis=0)
        scalars = jnp.concatenate(
            [jnp.stack([decay] + end_decays), request_prompt.astype(jnp.float32), jnp.zeros((3,), jnp.float32)]
        )
        small = jnp.broadcast_to(scalars[:, None], (8, 128))
        carried = jnp.where(segment == seg_before, jnp.exp(cum_log), 0.0)
        lines = jnp.stack(
            [cum_log, in_gate, segment.astype(jnp.float32), carried] + [jnp.zeros((tok_rows,), jnp.float32)] * 4
        )
        conv_act = lax.dynamic_slice_in_dim(head_act, col_idx * width, width, 1)
        gains = jnp.stack([norm_gain[layer], skip_gain[layer]])
        made = tail(
            sums, small, edges, lines, queries, key_rows, values, conv_act, outgate, gains, w_down[layer], current,
            layer + 1 < LAYERS,
        )
        current = made[0]
        states.append(made[1].reshape(2, 1, head_width, width))
        edges_out.append(made[2][:, : CONV - 1].astype(jnp.bfloat16))
        if layer + 1 < LAYERS:
            gathered = made[3]
    return (current, jnp.stack(states), jnp.stack(edges_out))


def solution(mesh):
    return jax.shard_map(
        body,
        mesh=mesh,
        in_specs=(
            P("seq", ("wr", "wc")),
            P(),
            P(None, None, ("wr", "wc")),
            P(None, None, ("wr", "wc")),
            P(),
            P(),
            P(None, None, ("wr", "wc")),
            P(None, ("wr", "wc")),
            P(None, "wr", None, None, None),
            P(None, "wr", None, None, None),
            P(None, "wr", None, "wc", None),
            P(None, ("wr", "wc")),
            P(None, ("wr", "wc")),
            P(None, ("wr", "wc"), None),
            P(),
            P("seq"),
        ),
        out_specs=(
            P("seq", ("wr", "wc")),
            P(None, "seq", "wr", None, "wc"),
            P(None, "seq", None, ("wr", "wc")),
        ),
        check_vma=False,
    )
```

```python
import jax
import jax.numpy as jnp
from jax import lax
from jax.experimental import pallas as pl
from jax.experimental.pallas import tpu as pltpu
from jax.sharding import PartitionSpec as P

HEADS = 4
CONV = 4
LAYERS = 2
PROMPTS = 3
SEQ = 16
SPLIT = 7

EPSILON = 1e-05
GATE_CAP = 15.0
FEATURE_DIMS = (((1,), (1,)), ((), ()))
ROW_DIMS = (((0,), (0,)), ((), ()))
MESH = pl.DeviceIdType.MESH
VM = pl.BlockSpec(memory_space=pltpu.VMEM)
DMA = pltpu.SemaphoreType.DMA


def params(collective):
    return pltpu.CompilerParams(
        collective_id=collective, has_side_effects=True, vmem_limit_bytes=48 * 1024 * 1024
    )


def greet(peers):
    barrier = pltpu.get_barrier_semaphore()
    for peer in peers:
        pl.semaphore_signal(barrier, inc=1, device_id=peer, device_id_type=MESH)
    pl.semaphore_wait(barrier, len(peers))


def copy_to(source, target, send, recv, peer):
    made = pltpu.make_async_remote_copy(
        src_ref=source, dst_ref=target, send_sem=send, recv_sem=recv, device_id=peer, device_id_type=MESH
    )
    made.start()
    return made


def plane():
    row, col = lax.axis_index("wr"), lax.axis_index("wc")
    core = lax.rem(col, 2)
    cross = lax.rem(col + 2, 4)
    mate = col + 1 - 2 * core
    return row, col, core, cross, mate


def gather_plane(own_ref, out_ref, send, recv):
    row, col, core, cross, mate = plane()
    mate_cross = lax.rem(mate + 2, 4)
    width = own_ref.shape[1]

    def block(r, c):
        return out_ref.at[:, pl.ds(pl.multiple_of((r * 4 + c) * width, width), width)]

    def move(source, r, c, slot, peer):
        return copy_to(source, block(r, c), send.at[slot], recv.at[slot], peer)

    rows = [lax.rem(row + d, 4) for d in range(4)]
    back = [lax.rem(row + 4 - d, 4) for d in range(4)]
    sent = {}
    sent[0] = move(own_ref, row, col, 0, {"wc": cross})
    for d in (1, 3, 2):
        sent[d] = move(own_ref, row, col, d, {"wr": rows[d]})
    sent[7] = move(own_ref, row, col, 7, {"wc": mate})
    sent[0].wait_recv()
    for d in (1, 3, 2):
        sent[3 + d] = move(block(row, cross), row, cross, 3 + d, {"wr": rows[d]})
    sent[8] = move(block(row, cross), row, cross, 8, {"wc": mate})
    for d in (1, 3, 2):
        sent[d].wait_recv()
        sent[8 + d] = move(block(back[d], col), back[d], col, 8 + d, {"wc": mate})
    for d in (1, 3, 2):
        sent[3 + d].wait_recv()
        sent[11 + d] = move(block(back[d], cross), back[d], cross, 11 + d, {"wc": mate})
    for slot in range(7, 15):
        sent[slot].wait_recv()
    for slot in range(15):
        sent[slot].wait_send()


def gather16(own, taps):
    rows, width = own.shape
    deep, share = taps.shape

    def kernel(own_ref, taps_ref, out_ref, all_ref, send, recv, tsend, trecv):
        row, col, core, cross, mate = plane()
        around = [{"wc": lax.rem(col + d, 4)} for d in (1, 2, 3)]
        greet([{"wr": lax.rem(row + d, 4)} for d in (1, 2, 3)] + around)
        mine = pl.ds(pl.multiple_of(col * share, share), share)
        made = [copy_to(taps_ref, all_ref.at[:, mine], tsend.at[d], trecv.at[d], around[d]) for d in range(3)]
        all_ref[:, mine] = taps_ref[...]
        out_ref[:, pl.ds(pl.multiple_of((row * 4 + col) * width, width), width)] = own_ref[...]
        gather_plane(own_ref, out_ref, send, recv)
        for copy in made:
            copy.wait_recv()
        for copy in made:
            copy.wait_send()

    return pl.pallas_call(
        kernel,
        out_shape=(
            jax.ShapeDtypeStruct((rows, width * 16), own.dtype),
            jax.ShapeDtypeStruct((deep, share * 4), taps.dtype),
        ),
        in_specs=[VM, VM],
        out_specs=(VM, VM),
        scratch_shapes=[DMA((15,)), DMA((15,)), DMA((3,)), DMA((3,))],
        compiler_params=params(1),
        name="gather_tokens",
    )(own, taps)


def gather_head(branch):
    rows, width = branch.shape
    rim = 16

    def kernel(own_ref, out_ref, rim_ref, send, recv):
        row, col, core, cross, mate = plane()
        place = lax.axis_index("seq")
        after = lax.rem(place + 1, SEQ)
        onward = [{"seq": after, "wc": lax.rem(col + j, 4)} for j in range(4)]
        before = lax.rem(place + SEQ - 1, SEQ)
        greet([{"wc": cross}, {"wc": mate}] + [{"seq": before, "wc": lax.rem(col + j, 4)} for j in range(4)])

        def block(ref, c):
            return ref.at[:, pl.ds(pl.multiple_of(c * width, width), width)]

        over = copy_to(own_ref, block(out_ref, col), send.at[0], recv.at[0], {"wc": cross})
        side = copy_to(own_ref, block(out_ref, col), send.at[1], recv.at[1], {"wc": mate})
        tails = [
            copy_to(own_ref.at[pl.ds(rows - rim, rim)], block(rim_ref, col), send.at[3 + j], recv.at[3 + j], onward[j])
            for j in range(4)
        ]
        out_ref[:, pl.ds(pl.multiple_of(col * width, width), width)] = own_ref[...]
        over.wait_recv()
        last = copy_to(block(out_ref, cross), block(out_ref, cross), send.at[2], recv.at[2], {"wc": mate})
        side.wait_recv()
        for tail in tails:
            tail.wait_recv()
        last.wait_recv()
        for made in [over, side, last] + tails:
            made.wait_send()

    return pl.pallas_call(
        kernel,
        out_shape=(
            jax.ShapeDtypeStruct((rows, width * 4), branch.dtype),
            jax.ShapeDtypeStruct((rim, width * 4), branch.dtype),
        ),
        in_specs=[VM],
        out_specs=(VM, VM),
        scratch_shapes=[DMA((7,)), DMA((7,))],
        compiler_params=params(2),
        name="gather_head",
    )(branch)


def tail(sums, small, edges, lines, queries, keys, values, act, outgate, gains, w_down, current, gather):
    spans, part, wide = sums.shape
    cols = wide // 3
    rows, width = current.shape
    head_width = queries.shape[1]
    tile = 128
    tiles = rows // tile

    def kernel(
        sums_ref, small_ref, edges_ref, lines_ref, q_ref, k_ref, v_ref, act_ref, og_ref, gains_ref, down_ref, cur_ref,
        *refs,
    ):
        new_ref, req_ref, edge_ref = refs[:3]
        if gather:
            out_ref, gsend, grecv = refs[3], refs[-2], refs[-1]
            refs = refs[:3] + refs[4:-2]
        (got, got_a, twin, paired, got_b, got_small, got_edges, going, state_ref, total, chosen, upright, hidden, stat,
         got_stat, gated, term, near, held, far, last, pair, send, recv, esend, erecv, local) = refs[3:]
        place = lax.axis_index("seq")
        row, col, core, cross, mate = plane()
        peers = [lax.rem(place + d, SEQ) for d in range(SEQ)]
        wc_peers = [{"wc": lax.rem(col + d, 4)} for d in (1, 2, 3)]
        greet(
            [{"wr": lax.rem(row + d, 4)} for d in (1, 2, 3)] + wc_peers + [{"seq": peers[d]} for d in range(1, SEQ)]
        )
        inc, end_a, end_b = [pl.ds(i * cols, cols) for i in range(3)]
        sent = []
        arrive = []
        for d in range(1, SEQ):
            to = {"seq": peers[d]}
            arrive.append(copy_to(small_ref, got_small.at[place], send.at[0, d], recv.at[0, d], to))
            arrive.append(copy_to(sums_ref.at[peers[d], :, inc], got.at[place], send.at[1, d], recv.at[1, d], to))
        sent += arrive
        odd = lax.rem(place, 2)
        level = lax.div(place, 2)
        beside = {"seq": place + 1 - 2 * odd}
        twins = [
            copy_to(sums_ref.at[2 * i + 1 - odd, :, end_a], twin.at[i], send.at[2, 8 + i], recv.at[2, 8 + i], beside)
            for i in range(8)
        ]
        sent += twins
        own = [
            pltpu.make_async_copy(small_ref, got_small.at[place], local.at[0]),
            pltpu.make_async_copy(sums_ref.at[place, :, inc], got.at[place], local.at[1]),
            pltpu.make_async_copy(edges_ref, got_edges.at[place], local.at[3]),
        ]
        for made in own:
            made.start()

        upright[...] = jnp.transpose(
            jnp.concatenate([lines_ref[...], jnp.zeros((128 - lines_ref.shape[0], rows), jnp.float32)])
        )
        for r in range(tiles):
            at = pl.ds(r * tile, tile)
            seen = (r + 1) * tile
            scores = lax.dot_general(
                q_ref[at], k_ref[pl.ds(0, seen)], FEATURE_DIMS, preferred_element_type=jnp.float32
            )
            gap = upright[at, 0:1] - lines_ref[0:1, 0:seen] + lines_ref[1:2, 0:seen]
            early = (
                lax.broadcasted_iota(jnp.int32, (tile, seen), 0) + r * tile
                >= lax.broadcasted_iota(jnp.int32, (tile, seen), 1)
            )
            allowed = early & (upright[at, 2:3] == lines_ref[2:3, 0:seen])
            scores = scores * jnp.exp(jnp.where(allowed, gap, -jnp.inf))
            hidden[at] = jnp.dot(
                scores.astype(jnp.bfloat16), v_ref[pl.ds(0, seen)], preferred_element_type=jnp.float32
            )

        for made in own:
            made.wait()
        for made in arrive:
            made.wait_recv()

        def scalar(k, i):
            line = got_small[k, i : i + 1]
            return jnp.concatenate([line] * (cols // 128), axis=1)

        state = jnp.zeros((part, cols), jnp.float32)
        first = jnp.zeros((part, cols), jnp.float32)
        second = jnp.zeros((part, cols), jnp.float32)
        for k in range(SEQ):
            going[k] = state.astype(jnp.bfloat16)
            if k <= SPLIT:
                first = first + scalar(k, 1) * state
            if k >= SPLIT:
                second = second + scalar(k, 2) * state
            state = scalar(k, 0) * state + got[k].astype(jnp.float32)
        total[0] = first
        total[1] = second
        total[2] = state
        arrive = [
            copy_to(going.at[peers[d]], state_ref.at[place], send.at[3, d], recv.at[3, d], {"seq": peers[d]})
            for d in range(1, SEQ)
        ]
        sent += arrive
        state_ref[place] = going[place]
        for i in range(8):
            twins[i].wait_recv()
            mine = sums_ref[2 * i + odd, :, cols : 2 * cols]
            paired[i] = (mine.astype(jnp.float32) + twin[i].astype(jnp.float32)).astype(jnp.bfloat16)
        got_a[level] = paired[level]
        for made in arrive:
            made.wait_recv()
        late = []
        for d in range(1, 8):
            to = lax.rem(level + d, 8)
            late.append(
                copy_to(paired.at[to], got_a.at[level], send.at[2, d], recv.at[2, d], {"seq": 2 * to + odd})
            )
        for d in range(1, SEQ):
            late.append(copy_to(edges_ref, got_edges.at[place], send.at[5, d], recv.at[5, d], {"seq": peers[d]}))
        sent += late
        b_copies = [
            pltpu.make_async_remote_copy(
                src_ref=sums_ref.at[peers[d], :, end_b], dst_ref=got_b, send_sem=send.at[4, d], recv_sem=recv.at[4, 0],
                device_id={"seq": peers[d]}, device_id_type=MESH,
            )
            for d in range(1, SEQ)
        ]

        @pl.when(place == SPLIT)
        def _():
            for made in b_copies:
                made.start()
            made = pltpu.make_async_copy(sums_ref.at[place, :, end_b], got_b, local.at[4])
            made.start()
            made.wait()

        lane = lax.broadcasted_iota(jnp.int32, (tile, 128), 1)
        whole = state_ref[...].reshape(head_width, cols)
        for r in range(tiles):
            at = pl.ds(r * tile, tile)
            here = hidden[at] + upright[at, 3:4] * jnp.dot(q_ref[at], whole, preferred_element_type=jnp.float32)
            hidden[at] = here
            ones = jnp.sum(here, axis=1, keepdims=True)
            twos = jnp.sum(here * here, axis=1, keepdims=True)
            upright[at] = jnp.where(lane == 0, ones, jnp.where(lane == 1, twos, 0.0))
        stat[...] = jnp.transpose(upright[...])[0:8]
        arrive = [copy_to(stat, got_stat.at[d], esend.at[d], erecv.at[d], wc_peers[d]) for d in range(3)]
        sent += arrive
        for made in arrive:
            made.wait_recv()
        sums_all = stat[...] + got_stat[0] + got_stat[1] + got_stat[2]
        upright[...] = jnp.transpose(jnp.concatenate([sums_all, jnp.zeros((120, rows), jnp.float32)]))
        for r in range(tiles):
            at = pl.ds(r * tile, tile)
            mean = upright[at, 0:1] / head_width
            var = upright[at, 1:2] / head_width - mean * mean
            normal = (hidden[at] - mean) * lax.rsqrt(var + EPSILON)
            gate = og_ref[at]
            gated[at] = (
                (normal * gains_ref[0:1] + gains_ref[1:2] * act_ref[at].astype(jnp.float32)) * (gate * jax.nn.sigmoid(gate))
            ).astype(jnp.bfloat16)

        order = [2, 1, 3, 0]
        rows_to = [lax.rem(row + d, 4) for d in range(4)]
        first = []
        for d in order:
            term[d] = jnp.dot(
                gated[...], down_ref[:, pl.ds(pl.multiple_of(rows_to[d] * 4 * width, 4 * width), 4 * width)],
                preferred_element_type=jnp.float32,
            ).astype(jnp.bfloat16)
            for h in range(2):
                first.append(
                    copy_to(
                        term.at[d, :, pl.ds(pl.multiple_of((2 * h + 1 - core) * width, width), width)],
                        near.at[2 * d + h], send.at[6, 2 * d + h], recv.at[6, 2 * d + h], {"wc": mate},
                    )
                )
        for made in late:
            made.wait_recv()

        @pl.when(place != SPLIT)
        def _():
            b_copies[0].wait_recv()

        whole_a, whole_b, third = total[0], total[1] + got_b[...].astype(jnp.float32), total[2]
        edge = jnp.zeros((16, cols), jnp.float32)
        for k in range(SEQ):
            edge = edge + got_edges[k].astype(jnp.float32)
        for k in range(8):
            if 2 * k <= SPLIT:
                whole_a = whole_a + got_a[k].astype(jnp.float32)
            else:
                whole_b = whole_b + got_a[k].astype(jnp.float32)
        total[0] = whole_a
        total[1] = whole_b
        side = []
        for d in range(1, SEQ):
            for j in range(2):
                which = got_small[peers[d], 3 + j : 4 + j]
                which = jnp.concatenate([which] * (cols // 128), axis=1)
                chosen[peers[d], j] = jnp.where(
                    which == 0.0, total[0], jnp.where(which == 1.0, total[1], total[2])
                ).astype(jnp.bfloat16)
            side.append(
                copy_to(chosen.at[peers[d]], req_ref.at[:, place], send.at[7, d], recv.at[7, d], {"seq": peers[d]})
            )
        for j in range(2):
            which = small_ref[3 + j : 4 + j]
            which = jnp.concatenate([which] * (cols // 128), axis=1)
            req_ref[j, place] = jnp.where(
                which == 0.0, total[0], jnp.where(which == 1.0, total[1], total[2])
            ).astype(jnp.bfloat16)
            edge_ref[j, 0:3] = jnp.where(
                which == 0.0, edge[0:3], jnp.where(which == 1.0, edge[3:6], edge[6:9])
            )
        sent += side

        second = []
        for i, d in enumerate(order):
            for h in range(2):
                first[2 * i + h].wait_recv()
                block = term[d, :, pl.ds(pl.multiple_of((2 * h + core) * width, width), width)]
                whole = block.astype(jnp.float32) + near[2 * d + h].astype(jnp.float32)
                if d > 0:
                    held[2 * d + h] = whole.astype(jnp.bfloat16)
                else:
                    pair[h] = whole
            if d > 0:
                second.append(
                    copy_to(held.at[pl.ds(2 * d, 2)], far.at[d - 1], esend.at[4 + d], erecv.at[4 + d], {"wr": rows_to[d]})
                )
        sent += first + second

        for made in second:
            made.wait_recv()
        other = lax.rem(lax.div(col, 2) + 1, 2)
        for h in range(2):
            pair[h] = (
                pair[h]
                + far[0, h].astype(jnp.float32)
                + far[1, h].astype(jnp.float32)
                + far[2, h].astype(jnp.float32)
            )
        held[0] = pair[other].astype(jnp.bfloat16)
        final = copy_to(held.at[0], last, esend.at[4], erecv.at[4], {"wc": cross})
        sent.append(final)
        final.wait_recv()
        new_ref[...] = (
            cur_ref[...].astype(jnp.float32) + (pair[1 - other] + last[...].astype(jnp.float32))
        ).astype(jnp.bfloat16)
        if gather:
            out_ref[:, pl.ds(pl.multiple_of((row * 4 + col) * width, width), width)] = new_ref[...]
            gather_plane(new_ref, out_ref, gsend, grecv)
        for made in side:
            made.wait_recv()
        for made in sent:
            made.wait_send()

        @pl.when(place == SPLIT)
        def _():
            for made in b_copies:
                made.wait_send()

    b16, f32 = jnp.bfloat16, jnp.float32
    shapes = [
        jax.ShapeDtypeStruct((rows, width), b16),
        jax.ShapeDtypeStruct((2, spans, part, cols), b16),
        jax.ShapeDtypeStruct((2, 8, cols), f32),
    ]
    scratch = [
        pltpu.VMEM((spans, part, cols), b16),
        pltpu.VMEM((8, part, cols), b16),
        pltpu.VMEM((8, part, cols), b16),
        pltpu.VMEM((8, part, cols), b16),
        pltpu.VMEM((part, cols), b16),
        pltpu.VMEM((spans, 8, 128), f32),
        pltpu.VMEM((spans, 16, cols), b16),
        pltpu.VMEM((spans, part, cols), b16),
        pltpu.VMEM((spans, part, cols), b16),
        pltpu.VMEM((3, part, cols), f32),
        pltpu.VMEM((spans, 2, part, cols), b16),
        pltpu.VMEM((rows, 128), f32),
        pltpu.VMEM((rows, cols), f32),
        pltpu.VMEM((8, rows), f32),
        pltpu.VMEM((3, 8, rows), f32),
        pltpu.VMEM((rows, cols), b16),
        pltpu.VMEM((4, rows, 4 * width), b16),
        pltpu.VMEM((8, rows, width), b16),
        pltpu.VMEM((8, rows, width), b16),
        pltpu.VMEM((3, 2, rows, width), b16),
        pltpu.VMEM((rows, width), b16),
        pltpu.VMEM((2, rows, width), f32),
        DMA((8, SEQ)), DMA((8, SEQ)), DMA((8,)), DMA((8,)), DMA((5,)),
    ]
    if gather:
        shapes.append(jax.ShapeDtypeStruct((rows, width * 16), b16))
        scratch += [DMA((15,)), DMA((15,))]
    return pl.pallas_call(
        kernel,
        out_shape=tuple(shapes),
        in_specs=[VM] * 12,
        out_specs=(VM,) * len(shapes),
        scratch_shapes=scratch,
        compiler_params=params(5 if gather else 6),
        name="tail_gather" if gather else "tail_last",
    )(sums, small, edges, lines, queries, keys, values, act, outgate, gains, w_down, current)


def norm_rows(source, gain_row):
    widened = source.astype(jnp.float32)
    row_mean = jnp.mean(widened, axis=1, keepdims=True)
    row_var = jnp.mean(widened * widened, axis=1, keepdims=True) - row_mean * row_mean
    return ((widened - row_mean) * lax.rsqrt(row_var + EPSILON) * gain_row).astype(jnp.bfloat16)


def segment_of(positions, lengths):
    bound_one = lengths[0]
    bound_two = lengths[0] + lengths[1]
    return (positions >= bound_one).astype(jnp.int32) + (positions >= bound_two).astype(jnp.int32)


def conv_rows(extended, ext_segment, segment, weight, bias_row):
    row_count = segment.shape[0]
    widened = extended.astype(jnp.float32)
    summed = jnp.zeros((row_count, widened.shape[1]), jnp.float32) + bias_row
    for back_step in range(weight.shape[0]):
        low_row = weight.shape[0] - 1 - back_step
        keep_row = (ext_segment[low_row : low_row + row_count] == segment).astype(jnp.float32)
        summed = (
            summed + weight[back_step] * widened[low_row : low_row + row_count] * keep_row[:, None]
        )
    return jax.nn.silu(summed).astype(jnp.bfloat16)


def block_mix(source, weight):
    group = weight.shape[2]
    widened = source.astype(jnp.float32)
    blocks = [
        sum(widened[:, i * group : (i + 1) * group] * weight[i, j] for i in range(4))
        for j in range(weight.shape[1])
    ]
    return jnp.concatenate(blocks, axis=1) if len(blocks) > 1 else blocks[0]


def body(
    tokens, ln_gain, w_branch, w_outgate, w_gates, forget_bias, conv_weight, conv_bias, w_query, w_key, w_value,
    skip_gain, norm_gain, w_down, lengths, request_prompt,
):
    tok_rows = tokens.shape[0]
    seq_index = lax.axis_index("seq")
    head_idx = lax.axis_index("wr")
    col_idx = lax.axis_index("wc")
    row_offset = seq_index * tok_rows
    total_rows = tok_rows * SEQ
    positions = row_offset + jnp.arange(tok_rows, dtype=jnp.int32)
    segment = segment_of(positions, lengths)
    seg_before = jnp.where(row_offset > 0, segment_of(row_offset - 1, lengths), -1)
    rim_positions = row_offset - (CONV - 1) + jnp.arange(CONV - 1, dtype=jnp.int32)
    rim_segment = jnp.where(rim_positions >= 0, segment_of(rim_positions, lengths), -1)
    ext_segment = jnp.concatenate([rim_segment, segment])
    starts = [jnp.zeros((), jnp.int32), lengths[0], lengths[0] + lengths[1]]
    ends = [lengths[0] - 1, lengths[0] + lengths[1] - 1, jnp.zeros((), jnp.int32) + (total_rows - 1)]
    holders = [(end >= row_offset) & (end < row_offset + tok_rows) for end in ends]
    local_ends = [jnp.clip(end - row_offset, 0, tok_rows - 1) for end in ends]
    head_mask = (jnp.arange(HEADS, dtype=jnp.int32) == head_idx).astype(jnp.float32)
    row_order = jnp.arange(tok_rows)
    taps = jnp.concatenate(
        [conv_weight.reshape(LAYERS * CONV, -1), conv_bias, jnp.zeros((6, conv_bias.shape[1]), jnp.float32)], axis=0
    )
    current = tokens
    gathered, taps_all = gather16(tokens, taps)
    states = []
    edges_out = []
    for layer in range(LAYERS):
        normed = norm_rows(gathered, ln_gain[layer])
        branch = jnp.dot(normed, w_branch[layer], preferred_element_type=jnp.float32).astype(jnp.bfloat16)
        outgate = jnp.dot(normed, w_outgate[layer], preferred_element_type=jnp.float32)
        gate_pre = jnp.dot(normed, w_gates[layer], preferred_element_type=jnp.float32)
        input_pre = jnp.sum(gate_pre[:, :HEADS] * head_mask, axis=1)
        forget_pre = jnp.sum((gate_pre[:, HEADS:] + forget_bias[layer]) * head_mask, axis=1)
        in_gate = GATE_CAP * jnp.tanh(input_pre / GATE_CAP)
        log_forget = jax.nn.log_sigmoid(forget_pre)
        head_branch, rim = gather_head(branch)
        width = branch.shape[1]
        extended = jnp.concatenate([rim[rim.shape[0] - (CONV - 1) :], head_branch], axis=0)
        head_act = conv_rows(
            extended, ext_segment, segment, taps_all[layer * CONV : (layer + 1) * CONV], taps_all[LAYERS * CONV + layer]
        )
        head_width = head_act.shape[1]
        queries = block_mix(head_act, w_query[layer, 0]).astype(jnp.bfloat16)
        key_rows = (block_mix(head_act, w_key[layer, 0]) * head_width ** (-0.5)).astype(jnp.bfloat16)
        values = block_mix(head_branch, w_value[layer, 0]).astype(jnp.bfloat16)
        cum_log = jnp.cumsum(log_forget)
        end_cum = cum_log[tok_rows - 1]
        last_seg = segment[tok_rows - 1]
        grow = jnp.where(segment == last_seg, jnp.exp(end_cum - cum_log + in_gate), 0.0)
        decay = jnp.where(last_seg == seg_before, jnp.exp(end_cum), 0.0)
        end_weights = []
        end_decays = []
        for prompt in range(2):
            local_cum = cum_log[local_ends[prompt]]
            chosen = holders[prompt] & (segment == prompt) & (row_order <= local_ends[prompt])
            end_weights.append(jnp.exp(jnp.where(chosen, local_cum - cum_log + in_gate, -jnp.inf)))
            end_decays.append(jnp.where(holders[prompt] & (seg_before == prompt), jnp.exp(local_cum), 0.0))
        weight_a = jnp.where(seq_index <= SPLIT, end_weights[0], end_weights[1])
        weights = jnp.stack([grow, weight_a, end_weights[1]], axis=1)
        weighted = (values.astype(jnp.float32)[:, None, :] * weights[:, :, None]).astype(jnp.bfloat16)
        sums = lax.dot_general(
            key_rows, weighted.reshape(tok_rows, -1), ROW_DIMS, preferred_element_type=jnp.float32
        ).astype(jnp.bfloat16)
        sums = sums.reshape(SEQ, head_width // SEQ, 3 * width)
        own_extended = lax.dynamic_slice_in_dim(extended, col_idx * width, width, 1)
        edge_rows = []
        for prompt in range(PROMPTS):
            window = lax.dynamic_slice_in_dim(own_extended, local_ends[prompt] + 1, CONV - 1, 0)
            edge_pos = ends[prompt] - (CONV - 2) + jnp.arange(CONV - 1, dtype=jnp.int32)
            keep = (edge_pos >= starts[prompt]) & holders[prompt]
            edge_rows.append(jnp.where(keep[:, None], window, jnp.zeros_like(window)))
        edges = jnp.concatenate(edge_rows + [jnp.zeros((7, width), jnp.bfloat16)], axis=0)
        scalars = jnp.concatenate(
            [jnp.stack([decay] + end_decays), request_prompt.astype(jnp.float32), jnp.zeros((3,), jnp.float32)]
        )
        small = jnp.broadcast_to(scalars[:, None], (8, 128))
        carried = jnp.where(segment == seg_before, jnp.exp(cum_log), 0.0)
        lines = jnp.stack(
            [cum_log, in_gate, segment.astype(jnp.float32), carried] + [jnp.zeros((tok_rows,), jnp.float32)] * 4
        )
        conv_act = lax.dynamic_slice_in_dim(head_act, col_idx * width, width, 1)
        gains = jnp.stack([norm_gain[layer], skip_gain[layer]])
        made = tail(
            sums, small, edges, lines, queries, key_rows, values, conv_act, outgate, gains, w_down[layer], current,
            layer + 1 < LAYERS,
        )
        current = made[0]
        states.append(made[1].reshape(2, 1, head_width, width))
        edges_out.append(made[2][:, : CONV - 1].astype(jnp.bfloat16))
        if layer + 1 < LAYERS:
            gathered = made[3]
    return (current, jnp.stack(states), jnp.stack(edges_out))


def solution(mesh):
    return jax.shard_map(
        body,
        mesh=mesh,
        in_specs=(
            P("seq", ("wr", "wc")),
            P(),
            P(None, None, ("wr", "wc")),
            P(None, None, ("wr", "wc")),
            P(),
            P(),
            P(None, None, ("wr", "wc")),
            P(None, ("wr", "wc")),
            P(None, "wr", None, None, None),
            P(None, "wr", None, None, None),
            P(None, "wr", None, "wc", None),
            P(None, ("wr", "wc")),
            P(None, ("wr", "wc")),
            P(None, ("wr", "wc"), None),
            P(),
            P("seq"),
        ),
        out_specs=(
            P("seq", ("wr", "wc")),
            P(None, "seq", "wr", None, "wc"),
            P(None, "seq", None, ("wr", "wc")),
        ),
        check_vma=False,
    )
```

```python
import jax
import jax.numpy as jnp
from jax import lax
from jax.experimental import pallas as pl
from jax.experimental.pallas import tpu as pltpu
from jax.sharding import PartitionSpec as P

HEADS = 4
CONV = 4
LAYERS = 2
PROMPTS = 3
SEQ = 16
SPLIT = 7

EPSILON = 1e-05
GATE_CAP = 15.0
FEATURE_DIMS = (((1,), (1,)), ((), ()))
ROW_DIMS = (((0,), (0,)), ((), ()))
MESH = pl.DeviceIdType.MESH
VM = pl.BlockSpec(memory_space=pltpu.VMEM)
DMA = pltpu.SemaphoreType.DMA


def params(collective):
    return pltpu.CompilerParams(
        collective_id=collective, has_side_effects=True, vmem_limit_bytes=48 * 1024 * 1024
    )


def greet(peers):
    barrier = pltpu.get_barrier_semaphore()
    for peer in peers:
        pl.semaphore_signal(barrier, inc=1, device_id=peer, device_id_type=MESH)
    pl.semaphore_wait(barrier, len(peers))


def copy_to(source, target, send, recv, peer):
    made = pltpu.make_async_remote_copy(
        src_ref=source, dst_ref=target, send_sem=send, recv_sem=recv, device_id=peer, device_id_type=MESH
    )
    made.start()
    return made


def plane():
    row, col = lax.axis_index("wr"), lax.axis_index("wc")
    core = lax.rem(col, 2)
    cross = lax.rem(col + 2, 4)
    mate = col + 1 - 2 * core
    return row, col, core, cross, mate


def gather_plane(own_ref, out_ref, send, recv):
    row, col, core, cross, mate = plane()
    mate_cross = lax.rem(mate + 2, 4)
    width = own_ref.shape[1]

    def block(r, c):
        return out_ref.at[:, pl.ds(pl.multiple_of((r * 4 + c) * width, width), width)]

    def move(source, r, c, slot, peer):
        return copy_to(source, block(r, c), send.at[slot], recv.at[slot], peer)

    rows = [lax.rem(row + d, 4) for d in range(4)]
    back = [lax.rem(row + 4 - d, 4) for d in range(4)]
    sent = {}
    sent[0] = move(own_ref, row, col, 0, {"wc": cross})
    for d in (1, 3, 2):
        sent[d] = move(own_ref, row, col, d, {"wr": rows[d]})
    sent[7] = move(own_ref, row, col, 7, {"wc": mate})
    sent[0].wait_recv()
    for d in (1, 3, 2):
        sent[3 + d] = move(block(row, cross), row, cross, 3 + d, {"wr": rows[d]})
    sent[8] = move(block(row, cross), row, cross, 8, {"wc": mate})
    for d in (1, 3, 2):
        sent[d].wait_recv()
        sent[8 + d] = move(block(back[d], col), back[d], col, 8 + d, {"wc": mate})
    for d in (1, 3, 2):
        sent[3 + d].wait_recv()
        sent[11 + d] = move(block(back[d], cross), back[d], cross, 11 + d, {"wc": mate})
    for slot in range(7, 15):
        sent[slot].wait_recv()
    for slot in range(15):
        sent[slot].wait_send()


def gather16(own, taps):
    rows, width = own.shape
    deep, share = taps.shape

    def kernel(own_ref, taps_ref, out_ref, all_ref, send, recv, tsend, trecv):
        row, col, core, cross, mate = plane()
        around = [{"wc": lax.rem(col + d, 4)} for d in (1, 2, 3)]
        greet([{"wr": lax.rem(row + d, 4)} for d in (1, 2, 3)] + around)
        mine = pl.ds(pl.multiple_of(col * share, share), share)
        made = [copy_to(taps_ref, all_ref.at[:, mine], tsend.at[d], trecv.at[d], around[d]) for d in range(3)]
        all_ref[:, mine] = taps_ref[...]
        out_ref[:, pl.ds(pl.multiple_of((row * 4 + col) * width, width), width)] = own_ref[...]
        gather_plane(own_ref, out_ref, send, recv)
        for copy in made:
            copy.wait_recv()
        for copy in made:
            copy.wait_send()

    return pl.pallas_call(
        kernel,
        out_shape=(
            jax.ShapeDtypeStruct((rows, width * 16), own.dtype),
            jax.ShapeDtypeStruct((deep, share * 4), taps.dtype),
        ),
        in_specs=[VM, VM],
        out_specs=(VM, VM),
        scratch_shapes=[DMA((15,)), DMA((15,)), DMA((3,)), DMA((3,))],
        compiler_params=params(1),
        name="gather_tokens",
    )(own, taps)


def gather_head(branch):
    rows, width = branch.shape
    rim = 16

    def kernel(own_ref, out_ref, rim_ref, send, recv):
        row, col, core, cross, mate = plane()
        place = lax.axis_index("seq")
        after = lax.rem(place + 1, SEQ)
        onward = [{"seq": after, "wc": lax.rem(col + j, 4)} for j in range(4)]
        before = lax.rem(place + SEQ - 1, SEQ)
        greet([{"wc": cross}, {"wc": mate}] + [{"seq": before, "wc": lax.rem(col + j, 4)} for j in range(4)])

        def block(ref, c):
            return ref.at[:, pl.ds(pl.multiple_of(c * width, width), width)]

        over = copy_to(own_ref, block(out_ref, col), send.at[0], recv.at[0], {"wc": cross})
        side = copy_to(own_ref, block(out_ref, col), send.at[1], recv.at[1], {"wc": mate})
        tails = [
            copy_to(own_ref.at[pl.ds(rows - rim, rim)], block(rim_ref, col), send.at[3 + j], recv.at[3 + j], onward[j])
            for j in range(4)
        ]
        out_ref[:, pl.ds(pl.multiple_of(col * width, width), width)] = own_ref[...]
        over.wait_recv()
        last = copy_to(block(out_ref, cross), block(out_ref, cross), send.at[2], recv.at[2], {"wc": mate})
        side.wait_recv()
        for tail in tails:
            tail.wait_recv()
        last.wait_recv()
        for made in [over, side, last] + tails:
            made.wait_send()

    return pl.pallas_call(
        kernel,
        out_shape=(
            jax.ShapeDtypeStruct((rows, width * 4), branch.dtype),
            jax.ShapeDtypeStruct((rim, width * 4), branch.dtype),
        ),
        in_specs=[VM],
        out_specs=(VM, VM),
        scratch_shapes=[DMA((7,)), DMA((7,))],
        compiler_params=params(2),
        name="gather_head",
    )(branch)


def tail(sums, small, edges, lines, queries, keys, values, act, outgate, gains, w_down, current, gather):
    spans, part, wide = sums.shape
    cols = wide // 3
    rows, width = current.shape
    head_width = queries.shape[1]
    tile = 128
    tiles = rows // tile

    def kernel(
        sums_ref, small_ref, edges_ref, lines_ref, q_ref, k_ref, v_ref, act_ref, og_ref, gains_ref, down_ref, cur_ref,
        *refs,
    ):
        new_ref, req_ref, edge_ref = refs[:3]
        if gather:
            out_ref, gsend, grecv = refs[3], refs[-2], refs[-1]
            refs = refs[:3] + refs[4:-2]
        (got, got_a, twin, paired, got_b, got_small, got_edges, going, state_ref, total, chosen, upright, hidden, stat,
         got_stat, gated, term, near, held, far, last, pair, send, recv, esend, erecv, local) = refs[3:]
        place = lax.axis_index("seq")
        row, col, core, cross, mate = plane()
        peers = [lax.rem(place + d, SEQ) for d in range(SEQ)]
        wc_peers = [{"wc": lax.rem(col + d, 4)} for d in (1, 2, 3)]
        greet(
            [{"wr": lax.rem(row + d, 4)} for d in (1, 2, 3)] + wc_peers + [{"seq": peers[d]} for d in range(1, SEQ)]
        )
        inc, end_a, end_b = [pl.ds(i * cols, cols) for i in range(3)]
        sent = []
        arrive = []
        for d in range(1, SEQ):
            to = {"seq": peers[d]}
            arrive.append(copy_to(small_ref, got_small.at[place], send.at[0, d], recv.at[0, d], to))
            arrive.append(copy_to(sums_ref.at[peers[d], :, inc], got.at[place], send.at[1, d], recv.at[1, d], to))
        sent += arrive
        odd = lax.rem(place, 2)
        level = lax.div(place, 2)
        beside = {"seq": place + 1 - 2 * odd}
        twins = [
            copy_to(sums_ref.at[2 * i + 1 - odd, :, end_a], twin.at[i], send.at[2, 8 + i], recv.at[2, 8 + i], beside)
            for i in range(8)
        ]
        sent += twins
        own = [
            pltpu.make_async_copy(small_ref, got_small.at[place], local.at[0]),
            pltpu.make_async_copy(sums_ref.at[place, :, inc], got.at[place], local.at[1]),
            pltpu.make_async_copy(edges_ref, got_edges.at[place], local.at[3]),
        ]
        for made in own:
            made.start()

        upright[...] = jnp.transpose(
            jnp.concatenate([lines_ref[...], jnp.zeros((128 - lines_ref.shape[0], rows), jnp.float32)])
        )
        for r in range(tiles):
            at = pl.ds(r * tile, tile)
            seen = (r + 1) * tile
            scores = lax.dot_general(
                q_ref[at], k_ref[pl.ds(0, seen)], FEATURE_DIMS, preferred_element_type=jnp.float32
            )
            gap = upright[at, 0:1] - lines_ref[0:1, 0:seen] + lines_ref[1:2, 0:seen]
            early = (
                lax.broadcasted_iota(jnp.int32, (tile, seen), 0) + r * tile
                >= lax.broadcasted_iota(jnp.int32, (tile, seen), 1)
            )
            allowed = early & (upright[at, 2:3] == lines_ref[2:3, 0:seen])
            scores = scores * jnp.exp(jnp.where(allowed, gap, -jnp.inf))
            hidden[at] = jnp.dot(
                scores.astype(jnp.bfloat16), v_ref[pl.ds(0, seen)], preferred_element_type=jnp.float32
            )

        for made in own:
            made.wait()
        for made in arrive:
            made.wait_recv()

        def scalar(k, i):
            line = got_small[k, i : i + 1]
            return jnp.concatenate([line] * (cols // 128), axis=1)

        state = jnp.zeros((part, cols), jnp.float32)
        first = jnp.zeros((part, cols), jnp.float32)
        second = jnp.zeros((part, cols), jnp.float32)
        for k in range(SEQ):
            going[k] = state.astype(jnp.bfloat16)
            if k <= SPLIT:
                first = first + scalar(k, 1) * state
            if k >= SPLIT:
                second = second + scalar(k, 2) * state
            state = scalar(k, 0) * state + got[k].astype(jnp.float32)
        total[0] = first
        total[1] = second
        total[2] = state
        arrive = [
            copy_to(going.at[peers[d]], state_ref.at[place], send.at[3, d], recv.at[3, d], {"seq": peers[d]})
            for d in range(1, SEQ)
        ]
        sent += arrive
        state_ref[place] = going[place]
        for i in range(8):
            twins[i].wait_recv()
            mine = sums_ref[2 * i + odd, :, cols : 2 * cols]
            paired[i] = (mine.astype(jnp.float32) + twin[i].astype(jnp.float32)).astype(jnp.bfloat16)
        got_a[level] = paired[level]
        for made in arrive:
            made.wait_recv()
        late = []
        for d in range(1, 8):
            to = lax.rem(level + d, 8)
            late.append(
                copy_to(paired.at[to], got_a.at[level], send.at[2, d], recv.at[2, d], {"seq": 2 * to + odd})
            )
        for d in range(1, SEQ):
            late.append(copy_to(edges_ref, got_edges.at[place], send.at[5, d], recv.at[5, d], {"seq": peers[d]}))
        sent += late
        b_copies = [
            pltpu.make_async_remote_copy(
                src_ref=sums_ref.at[peers[d], :, end_b], dst_ref=got_b, send_sem=send.at[4, d], recv_sem=recv.at[4, 0],
                device_id={"seq": peers[d]}, device_id_type=MESH,
            )
            for d in range(1, SEQ)
        ]

        @pl.when(place == SPLIT)
        def _():
            for made in b_copies:
                made.start()
            made = pltpu.make_async_copy(sums_ref.at[place, :, end_b], got_b, local.at[4])
            made.start()
            made.wait()

        lane = lax.broadcasted_iota(jnp.int32, (tile, 128), 1)
        whole = state_ref[...].reshape(head_width, cols)
        for r in range(tiles):
            at = pl.ds(r * tile, tile)
            here = hidden[at] + upright[at, 3:4] * jnp.dot(q_ref[at], whole, preferred_element_type=jnp.float32)
            hidden[at] = here
            ones = jnp.sum(here, axis=1, keepdims=True)
            twos = jnp.sum(here * here, axis=1, keepdims=True)
            upright[at] = jnp.where(lane == 0, ones, jnp.where(lane == 1, twos, 0.0))
        stat[...] = jnp.transpose(upright[...])[0:8]
        arrive = [copy_to(stat, got_stat.at[d], esend.at[d], erecv.at[d], wc_peers[d]) for d in range(3)]
        sent += arrive
        for made in arrive:
            made.wait_recv()
        sums_all = stat[...] + got_stat[0] + got_stat[1] + got_stat[2]
        upright[...] = jnp.transpose(jnp.concatenate([sums_all, jnp.zeros((120, rows), jnp.float32)]))
        for r in range(tiles):
            at = pl.ds(r * tile, tile)
            mean = upright[at, 0:1] / head_width
            var = upright[at, 1:2] / head_width - mean * mean
            normal = (hidden[at] - mean) * lax.rsqrt(var + EPSILON)
            gate = og_ref[at]
            gated[at] = (
                (normal * gains_ref[0:1] + gains_ref[1:2] * act_ref[at].astype(jnp.float32)) * (gate * jax.nn.sigmoid(gate))
            ).astype(jnp.bfloat16)

        def deliver():
            for made in late:
                made.wait_recv()

            @pl.when(place != SPLIT)
            def _():
                b_copies[0].wait_recv()

            whole_a, whole_b, third = total[0], total[1] + got_b[...].astype(jnp.float32), total[2]
            edge = jnp.zeros((16, cols), jnp.float32)
            for k in range(SEQ):
                edge = edge + got_edges[k].astype(jnp.float32)
            for k in range(8):
                if 2 * k <= SPLIT:
                    whole_a = whole_a + got_a[k].astype(jnp.float32)
                else:
                    whole_b = whole_b + got_a[k].astype(jnp.float32)
            total[0] = whole_a
            total[1] = whole_b
            side = []
            for d in range(1, SEQ):
                for j in range(2):
                    which = got_small[peers[d], 3 + j : 4 + j]
                    which = jnp.concatenate([which] * (cols // 128), axis=1)
                    chosen[peers[d], j] = jnp.where(
                        which == 0.0, total[0], jnp.where(which == 1.0, total[1], total[2])
                    ).astype(jnp.bfloat16)
                side.append(
                    copy_to(chosen.at[peers[d]], req_ref.at[:, place], send.at[7, d], recv.at[7, d], {"seq": peers[d]})
                )
            for j in range(2):
                which = small_ref[3 + j : 4 + j]
                which = jnp.concatenate([which] * (cols // 128), axis=1)
                req_ref[j, place] = jnp.where(
                    which == 0.0, total[0], jnp.where(which == 1.0, total[1], total[2])
                ).astype(jnp.bfloat16)
                edge_ref[j, 0:3] = jnp.where(
                    which == 0.0, edge[0:3], jnp.where(which == 1.0, edge[3:6], edge[6:9])
                )
            return side

        order = [2, 1, 3, 0]
        rows_to = [lax.rem(row + d, 4) for d in range(4)]
        first = []
        for d in order:
            term[d] = jnp.dot(
                gated[...], down_ref[:, pl.ds(pl.multiple_of(rows_to[d] * 4 * width, 4 * width), 4 * width)],
                preferred_element_type=jnp.float32,
            ).astype(jnp.bfloat16)
            for h in range(2):
                first.append(
                    copy_to(
                        term.at[d, :, pl.ds(pl.multiple_of((2 * h + 1 - core) * width, width), width)],
                        near.at[2 * d + h], send.at[6, 2 * d + h], recv.at[6, 2 * d + h], {"wc": mate},
                    )
                )
        side = [] if gather else deliver()
        second = []
        for i, d in enumerate(order):
            for h in range(2):
                first[2 * i + h].wait_recv()
                block = term[d, :, pl.ds(pl.multiple_of((2 * h + core) * width, width), width)]
                whole = block.astype(jnp.float32) + near[2 * d + h].astype(jnp.float32)
                if d > 0:
                    held[2 * d + h] = whole.astype(jnp.bfloat16)
                else:
                    pair[h] = whole
            if d > 0:
                second.append(
                    copy_to(held.at[pl.ds(2 * d, 2)], far.at[d - 1], esend.at[4 + d], erecv.at[4 + d], {"wr": rows_to[d]})
                )
        sent += first + second

        if gather:
            side = deliver()
        sent += side
        for made in second:
            made.wait_recv()
        other = lax.rem(lax.div(col, 2) + 1, 2)
        for h in range(2):
            pair[h] = (
                pair[h]
                + far[0, h].astype(jnp.float32)
                + far[1, h].astype(jnp.float32)
                + far[2, h].astype(jnp.float32)
            )
        held[0] = pair[other].astype(jnp.bfloat16)
        final = copy_to(held.at[0], last, esend.at[4], erecv.at[4], {"wc": cross})
        sent.append(final)
        final.wait_recv()
        new_ref[...] = (
            cur_ref[...].astype(jnp.float32) + (pair[1 - other] + last[...].astype(jnp.float32))
        ).astype(jnp.bfloat16)
        if gather:
            out_ref[:, pl.ds(pl.multiple_of((row * 4 + col) * width, width), width)] = new_ref[...]
            gather_plane(new_ref, out_ref, gsend, grecv)
        for made in side:
            made.wait_recv()
        for made in sent:
            made.wait_send()

        @pl.when(place == SPLIT)
        def _():
            for made in b_copies:
                made.wait_send()

    b16, f32 = jnp.bfloat16, jnp.float32
    shapes = [
        jax.ShapeDtypeStruct((rows, width), b16),
        jax.ShapeDtypeStruct((2, spans, part, cols), b16),
        jax.ShapeDtypeStruct((2, 8, cols), f32),
    ]
    scratch = [
        pltpu.VMEM((spans, part, cols), b16),
        pltpu.VMEM((8, part, cols), b16),
        pltpu.VMEM((8, part, cols), b16),
        pltpu.VMEM((8, part, cols), b16),
        pltpu.VMEM((part, cols), b16),
        pltpu.VMEM((spans, 8, 128), f32),
        pltpu.VMEM((spans, 16, cols), b16),
        pltpu.VMEM((spans, part, cols), b16),
        pltpu.VMEM((spans, part, cols), b16),
        pltpu.VMEM((3, part, cols), f32),
        pltpu.VMEM((spans, 2, part, cols), b16),
        pltpu.VMEM((rows, 128), f32),
        pltpu.VMEM((rows, cols), f32),
        pltpu.VMEM((8, rows), f32),
        pltpu.VMEM((3, 8, rows), f32),
        pltpu.VMEM((rows, cols), b16),
        pltpu.VMEM((4, rows, 4 * width), b16),
        pltpu.VMEM((8, rows, width), b16),
        pltpu.VMEM((8, rows, width), b16),
        pltpu.VMEM((3, 2, rows, width), b16),
        pltpu.VMEM((rows, width), b16),
        pltpu.VMEM((2, rows, width), f32),
        DMA((8, SEQ)), DMA((8, SEQ)), DMA((8,)), DMA((8,)), DMA((5,)),
    ]
    if gather:
        shapes.append(jax.ShapeDtypeStruct((rows, width * 16), b16))
        scratch += [DMA((15,)), DMA((15,))]
    return pl.pallas_call(
        kernel,
        out_shape=tuple(shapes),
        in_specs=[VM] * 12,
        out_specs=(VM,) * len(shapes),
        scratch_shapes=scratch,
        compiler_params=params(5 if gather else 6),
        name="tail_gather" if gather else "tail_last",
    )(sums, small, edges, lines, queries, keys, values, act, outgate, gains, w_down, current)


def norm_rows(source, gain_row):
    widened = source.astype(jnp.float32)
    row_mean = jnp.mean(widened, axis=1, keepdims=True)
    row_var = jnp.mean(widened * widened, axis=1, keepdims=True) - row_mean * row_mean
    return ((widened - row_mean) * lax.rsqrt(row_var + EPSILON) * gain_row).astype(jnp.bfloat16)


def segment_of(positions, lengths):
    bound_one = lengths[0]
    bound_two = lengths[0] + lengths[1]
    return (positions >= bound_one).astype(jnp.int32) + (positions >= bound_two).astype(jnp.int32)


def conv_rows(extended, ext_segment, segment, weight, bias_row):
    row_count = segment.shape[0]
    widened = extended.astype(jnp.float32)
    summed = jnp.zeros((row_count, widened.shape[1]), jnp.float32) + bias_row
    for back_step in range(weight.shape[0]):
        low_row = weight.shape[0] - 1 - back_step
        keep_row = (ext_segment[low_row : low_row + row_count] == segment).astype(jnp.float32)
        summed = (
            summed + weight[back_step] * widened[low_row : low_row + row_count] * keep_row[:, None]
        )
    return jax.nn.silu(summed).astype(jnp.bfloat16)


def block_mix(source, weight):
    group = weight.shape[2]
    widened = source.astype(jnp.float32)
    blocks = [
        sum(widened[:, i * group : (i + 1) * group] * weight[i, j] for i in range(4))
        for j in range(weight.shape[1])
    ]
    return jnp.concatenate(blocks, axis=1) if len(blocks) > 1 else blocks[0]


def body(
    tokens, ln_gain, w_branch, w_outgate, w_gates, forget_bias, conv_weight, conv_bias, w_query, w_key, w_value,
    skip_gain, norm_gain, w_down, lengths, request_prompt,
):
    tok_rows = tokens.shape[0]
    seq_index = lax.axis_index("seq")
    head_idx = lax.axis_index("wr")
    col_idx = lax.axis_index("wc")
    row_offset = seq_index * tok_rows
    total_rows = tok_rows * SEQ
    positions = row_offset + jnp.arange(tok_rows, dtype=jnp.int32)
    segment = segment_of(positions, lengths)
    seg_before = jnp.where(row_offset > 0, segment_of(row_offset - 1, lengths), -1)
    rim_positions = row_offset - (CONV - 1) + jnp.arange(CONV - 1, dtype=jnp.int32)
    rim_segment = jnp.where(rim_positions >= 0, segment_of(rim_positions, lengths), -1)
    ext_segment = jnp.concatenate([rim_segment, segment])
    starts = [jnp.zeros((), jnp.int32), lengths[0], lengths[0] + lengths[1]]
    ends = [lengths[0] - 1, lengths[0] + lengths[1] - 1, jnp.zeros((), jnp.int32) + (total_rows - 1)]
    holders = [(end >= row_offset) & (end < row_offset + tok_rows) for end in ends]
    local_ends = [jnp.clip(end - row_offset, 0, tok_rows - 1) for end in ends]
    head_mask = (jnp.arange(HEADS, dtype=jnp.int32) == head_idx).astype(jnp.float32)
    row_order = jnp.arange(tok_rows)
    taps = jnp.concatenate(
        [conv_weight.reshape(LAYERS * CONV, -1), conv_bias, jnp.zeros((6, conv_bias.shape[1]), jnp.float32)], axis=0
    )
    current = tokens
    gathered, taps_all = gather16(tokens, taps)
    states = []
    edges_out = []
    for layer in range(LAYERS):
        normed = norm_rows(gathered, ln_gain[layer])
        branch = jnp.dot(normed, w_branch[layer], preferred_element_type=jnp.float32).astype(jnp.bfloat16)
        outgate = jnp.dot(normed, w_outgate[layer], preferred_element_type=jnp.float32)
        gate_pre = jnp.dot(normed, w_gates[layer], preferred_element_type=jnp.float32)
        input_pre = jnp.sum(gate_pre[:, :HEADS] * head_mask, axis=1)
        forget_pre = jnp.sum((gate_pre[:, HEADS:] + forget_bias[layer]) * head_mask, axis=1)
        in_gate = GATE_CAP * jnp.tanh(input_pre / GATE_CAP)
        log_forget = jax.nn.log_sigmoid(forget_pre)
        head_branch, rim = gather_head(branch)
        width = branch.shape[1]
        extended = jnp.concatenate([rim[rim.shape[0] - (CONV - 1) :], head_branch], axis=0)
        head_act = conv_rows(
            extended, ext_segment, segment, taps_all[layer * CONV : (layer + 1) * CONV], taps_all[LAYERS * CONV + layer]
        )
        head_width = head_act.shape[1]
        queries = block_mix(head_act, w_query[layer, 0]).astype(jnp.bfloat16)
        key_rows = (block_mix(head_act, w_key[layer, 0]) * head_width ** (-0.5)).astype(jnp.bfloat16)
        values = block_mix(head_branch, w_value[layer, 0]).astype(jnp.bfloat16)
        cum_log = jnp.cumsum(log_forget)
        end_cum = cum_log[tok_rows - 1]
        last_seg = segment[tok_rows - 1]
        grow = jnp.where(segment == last_seg, jnp.exp(end_cum - cum_log + in_gate), 0.0)
        decay = jnp.where(last_seg == seg_before, jnp.exp(end_cum), 0.0)
        end_weights = []
        end_decays = []
        for prompt in range(2):
            local_cum = cum_log[local_ends[prompt]]
            chosen = holders[prompt] & (segment == prompt) & (row_order <= local_ends[prompt])
            end_weights.append(jnp.exp(jnp.where(chosen, local_cum - cum_log + in_gate, -jnp.inf)))
            end_decays.append(jnp.where(holders[prompt] & (seg_before == prompt), jnp.exp(local_cum), 0.0))
        weight_a = jnp.where(seq_index <= SPLIT, end_weights[0], end_weights[1])
        weights = jnp.stack([grow, weight_a, end_weights[1]], axis=1)
        weighted = (values.astype(jnp.float32)[:, None, :] * weights[:, :, None]).astype(jnp.bfloat16)
        sums = lax.dot_general(
            key_rows, weighted.reshape(tok_rows, -1), ROW_DIMS, preferred_element_type=jnp.float32
        ).astype(jnp.bfloat16)
        sums = sums.reshape(SEQ, head_width // SEQ, 3 * width)
        own_extended = lax.dynamic_slice_in_dim(extended, col_idx * width, width, 1)
        edge_rows = []
        for prompt in range(PROMPTS):
            window = lax.dynamic_slice_in_dim(own_extended, local_ends[prompt] + 1, CONV - 1, 0)
            edge_pos = ends[prompt] - (CONV - 2) + jnp.arange(CONV - 1, dtype=jnp.int32)
            keep = (edge_pos >= starts[prompt]) & holders[prompt]
            edge_rows.append(jnp.where(keep[:, None], window, jnp.zeros_like(window)))
        edges = jnp.concatenate(edge_rows + [jnp.zeros((7, width), jnp.bfloat16)], axis=0)
        scalars = jnp.concatenate(
            [jnp.stack([decay] + end_decays), request_prompt.astype(jnp.float32), jnp.zeros((3,), jnp.float32)]
        )
        small = jnp.broadcast_to(scalars[:, None], (8, 128))
        carried = jnp.where(segment == seg_before, jnp.exp(cum_log), 0.0)
        lines = jnp.stack(
            [cum_log, in_gate, segment.astype(jnp.float32), carried] + [jnp.zeros((tok_rows,), jnp.float32)] * 4
        )
        conv_act = lax.dynamic_slice_in_dim(head_act, col_idx * width, width, 1)
        gains = jnp.stack([norm_gain[layer], skip_gain[layer]])
        made = tail(
            sums, small, edges, lines, queries, key_rows, values, conv_act, outgate, gains, w_down[layer], current,
            layer + 1 < LAYERS,
        )
        current = made[0]
        states.append(made[1].reshape(2, 1, head_width, width))
        edges_out.append(made[2][:, : CONV - 1].astype(jnp.bfloat16))
        if layer + 1 < LAYERS:
            gathered = made[3]
    return (current, jnp.stack(states), jnp.stack(edges_out))


def solution(mesh):
    return jax.shard_map(
        body,
        mesh=mesh,
        in_specs=(
            P("seq", ("wr", "wc")),
            P(),
            P(None, None, ("wr", "wc")),
            P(None, None, ("wr", "wc")),
            P(),
            P(),
            P(None, None, ("wr", "wc")),
            P(None, ("wr", "wc")),
            P(None, "wr", None, None, None),
            P(None, "wr", None, None, None),
            P(None, "wr", None, "wc", None),
            P(None, ("wr", "wc")),
            P(None, ("wr", "wc")),
            P(None, ("wr", "wc"), None),
            P(),
            P("seq"),
        ),
        out_specs=(
            P("seq", ("wr", "wc")),
            P(None, "seq", "wr", None, "wc"),
            P(None, "seq", None, ("wr", "wc")),
        ),
        check_vma=False,
    )
```
